128 devices in a mesh: seq: 16 (over y, z), batch: 8 (over x, core).
Axes of the slice: x: 4, y: 4, z: 4, core: 2. Of those that a mesh axis runs over, the one named last changes fastest.
Arguments:
- q_nope: bfloat16 [8, 64, 128, 128], P('batch', None, 'seq'), may hold values from -6 to 6
- q_rope: bfloat16 [8, 64, 128, 64], P('batch', None, 'seq'), may hold values from -8 to 8
- absorb_k: bfloat16 [128, 128, 512], P('seq'), may hold values from -0.5 to 0.5
- absorb_v: bfloat16 [128, 512, 128], P('seq'), may hold values from -0.25 to 0.25
- cache_latent: bfloat16 [8, 16384, 512], P('batch', 'seq'), may hold values from -6 to 6
- cache_rope: bfloat16 [8, 16384, 64], P('batch', 'seq'), may hold values from -8 to 8
- draft_latent: bfloat16 [8, 64, 512], P('batch'), may hold values from -6 to 6
- draft_rope: bfloat16 [8, 64, 64], P('batch'), may hold values from -6 to 6
- residual: bfloat16 [512, 7168], P('batch', 'seq'), may hold values from -1.2 to 1.2
- out_proj: bfloat16 [16384, 7168], P('seq'), may hold values from -0.046875 to 0.046875
- norm_gain: float32 [7168], replicated, may hold values from 0.5 to 1.5
- lm_head: bfloat16 [65536, 7168], P(('seq', 'batch')), may hold values from -2.4095235 to 2.4095235
- parent: int32 [8, 64], replicated, may hold values from 0 to 62, as said below
- draft_ids: int32 [8, 64], replicated, may hold values from 0 to 65535
- cache_len: int32 [8], P('batch'), may hold values from 4096 to 16384
- accept_len: int32 [8], P('batch'), may hold values from 1 to 64
Outputs:
- hidden_out: bfloat16 [512, 7168], P('batch', 'seq')
- target_logp: float32 [8, 64], P('batch')
- accepted_score: float32 [8], P('batch')
The draws below stay inside these ranges and needn't reach their ends.
Inputs may be any that keep to these rules, and one draw needn't show every extreme that they name: parent[b, 0] = 0, and 0 <= parent[b, i] < i for i >= 1.
All inputs are finite; a program needn't handle non-finite values.
Results may differ from the reference program's by a relative error of at most 0.0095.
Values may be sent and summed in bfloat16 or wider, within the bound.
A program may use at most 256 MiB of HBM per device.

```python
import math
import jax
import jax.numpy as jnp
from jax import lax

H = 128
HN = 128
HR = 64
C = 512
D = 7168
VOCAB = 65536
DRAFT = 64
REQUESTS = 8
LENGTH = 16384
TOKENS = 512


def draw_q_rope(key, part):
    full_shape = (REQUESTS, DRAFT, H, HR)
    values = jnp.clip(jax.random.normal(jax.random.fold_in(key, 11), full_shape, jnp.float32), -6.0, 6.0)
    return values.astype(jnp.bfloat16)


def draw_cache_rope(key, part):
    full_shape = (REQUESTS, LENGTH, HR)
    values = jnp.clip(jax.random.normal(jax.random.fold_in(key, 13), full_shape, jnp.float32), -6.0, 6.0)
    return values.astype(jnp.bfloat16)


def draw_residual(key, part):
    columns = jnp.arange(D, dtype=jnp.float32) / (D - 1)
    column_scale = 0.05 * (1.0 + 2.0 * columns)
    values = jnp.clip(jax.random.normal(jax.random.fold_in(key, 17), (TOKENS, D), jnp.float32), -6.0, 6.0)
    return (values * column_scale).astype(jnp.bfloat16)


def draw_lm_head(key, part):
    entries = jnp.arange(VOCAB, dtype=jnp.float32) / (VOCAB - 1)
    row_scale = (jnp.exp(jnp.log(3.0) * entries) / jnp.sqrt(jnp.float32(D)))[:, None]
    values = jnp.clip(jax.random.normal(jax.random.fold_in(key, 19), (VOCAB, D), jnp.float32), -6.0, 6.0) * row_scale
    return values.astype(jnp.bfloat16)


def draw_parent(key, part):
    choices_drawn = jax.random.randint(jax.random.fold_in(key, 3), (REQUESTS, DRAFT), 0, 1 << 20, dtype=jnp.int32)
    indices = jnp.arange(DRAFT, dtype=jnp.int32)
    spread = jnp.maximum(jnp.minimum(indices, 4), 1)
    parents = jnp.where(indices[None, :] == 0, 0, indices[None, :] - 1 - choices_drawn % spread[None, :])
    return parents.astype(jnp.int32)


def plant(array, key, low, largest):
    longest = array.shape.index(max(array.shape))
    spots = []
    for shift in (0, 1):
        where = [jax.random.randint(jax.random.fold_in(key, axis), (), 0, length) for axis, length in enumerate(array.shape)]
        where[longest] = (where[longest] + shift) % array.shape[longest]
        spots.append(tuple(where))
    return array.at[spots[0]].set(low).at[spots[1]].set(largest)


def block_scale(rng, dims, pieces, smallest, largest):
    loudness, own = 1.0, jax.random.fold_in(rng, 6)
    for dim, shards_of in pieces:
        steps = jnp.exp(jax.random.uniform(jax.random.fold_in(own, dim), (shards_of,), jnp.float32, smallest / len(pieces), largest / len(pieces)))
        loudness = loudness * jnp.repeat(steps, dims[dim] // shards_of).reshape([-1 if axis == dim else 1 for axis in range(len(dims))])
    return loudness


def normal_values(stream_key, dims, width, limit, cuts=(), held_as=jnp.bfloat16):
    level = block_scale(stream_key, dims, cuts, -0.22, 0.18) if cuts else 1.0
    values = jax.random.normal(stream_key, dims, jnp.float32) * width * level
    return jnp.minimum(jnp.maximum(values, -limit), limit).astype(held_as)


def setup_inputs(seed: int = 0) -> dict:
    seeds = jax.random.split(jax.random.key(seed), 17)
    q_nope = normal_values(seeds[0], (REQUESTS, DRAFT, H, HN), 1.0, 6.0, ((0, 8), (2, 16)))
    q_rope = draw_q_rope(jax.random.fold_in(seeds[16], 71), 0)
    absorb_k = normal_values(seeds[2], (H, HN, C), HN ** -0.5, 0.5, ((0, 16),))
    absorb_v = normal_values(seeds[3], (H, C, HN), C ** -0.5, 0.25, ((0, 16),))
    cache_latent = normal_values(seeds[4], (REQUESTS, LENGTH, C), 1.0, 6.0, ((0, 8), (1, 16)))
    cache_rope = draw_cache_rope(jax.random.fold_in(seeds[16], 71), 0)
    draft_latent = normal_values(seeds[6], (REQUESTS, DRAFT, C), 1.0, 6.0, ((0, 8),))
    draft_rope = normal_values(seeds[7], (REQUESTS, DRAFT, HR), 1.0, 6.0, ((0, 8),))
    residual = draw_residual(jax.random.fold_in(seeds[16], 71), 0)
    out_proj = normal_values(seeds[9], (H * HN, D), (H * HN) ** -0.5, 0.046875, ((0, 16),))
    norm_gain = jnp.clip(1.0 + 0.1 * jax.random.normal(seeds[10], (D,), jnp.float32), 0.5, 1.5)
    lm_head = draw_lm_head(jax.random.fold_in(seeds[16], 71), 0)
    parent = draw_parent(jax.random.fold_in(seeds[16], 71), 0)
    draft_ids = plant(jax.random.randint(seeds[13], (REQUESTS, DRAFT), 0, VOCAB), jax.random.fold_in(seeds[13], 1), 0, VOCAB - 1).astype(jnp.int32)
    cache_len = plant(jax.random.randint(seeds[14], (REQUESTS,), LENGTH // 4, LENGTH + 1), jax.random.fold_in(seeds[14], 1), LENGTH // 4, LENGTH).astype(jnp.int32)
    accept_len = plant(jax.random.randint(seeds[15], (REQUESTS,), 1, DRAFT + 1), jax.random.fold_in(seeds[15], 1), 1, DRAFT).astype(jnp.int32)
    return dict(q_nope=q_nope, q_rope=q_rope, absorb_k=absorb_k, absorb_v=absorb_v, cache_latent=cache_latent, cache_rope=cache_rope, draft_latent=draft_latent, draft_rope=draft_rope, residual=residual, out_proj=out_proj, norm_gain=norm_gain, lm_head=lm_head, parent=parent, draft_ids=draft_ids, cache_len=cache_len, accept_len=accept_len)


masked_value = -1e+30
norm_epsilon = 1e-06
highest = lax.Precision.HIGHEST

def ancestry_of(parents):
    draft_count = parents.shape[1]
    indices = jnp.arange(draft_count, dtype=jnp.int32)
    parent_map = ((parents[:, :, None] == indices[None, None, :]) & (indices[None, :, None] > 0)).astype(jnp.float32)
    ancestry = jnp.broadcast_to(jnp.eye(draft_count, dtype=jnp.float32), parent_map.shape)
    for doubling in range(draft_count.bit_length() - 1):
        ancestry = ancestry + jnp.einsum('rij,rjk->rik', ancestry, parent_map, precision=highest)
        parent_map = jnp.einsum('rij,rjk->rik', parent_map, parent_map, precision=highest)
    return ancestry > 0.5

def rounded(values):
    return lax.optimization_barrier(values.astype(jnp.bfloat16)).astype(jnp.float32)

def reference(q_nope, q_rope, absorb_k, absorb_v, cache_latent, cache_rope, draft_latent, draft_rope, residual, out_proj, norm_gain, lm_head, parent, draft_ids, cache_len, accept_len):
    score_scale = 1.0 / math.sqrt(HN + HR)
    ancestry = ancestry_of(parent)
    head_block = min(H, 16)
    absorb_k32 = absorb_k.astype(jnp.float32)
    absorb_v32 = absorb_v.astype(jnp.float32)

    def one_request(inputs):
        nope_query, rope_query, latent_cache, rope_cache, latent_draft, rope_draft, length, ancestors = inputs
        query_latent = rounded(jnp.einsum('ihn,hnc->ihc', nope_query.astype(jnp.float32), absorb_k32, precision=highest))
        rope_all = rope_query.astype(jnp.float32)
        latent32 = latent_cache.astype(jnp.float32)
        rope32 = rope_cache.astype(jnp.float32)
        draft32 = latent_draft.astype(jnp.float32)
        draft_rope32 = rope_draft.astype(jnp.float32)
        in_cache = jnp.arange(LENGTH, dtype=jnp.int32) < length

        def per_block(block_index):
            first = (block_index * head_block).astype(jnp.int32)
            query_part = lax.dynamic_slice_in_dim(query_latent, first, head_block, 1)
            rope_part = lax.dynamic_slice_in_dim(rope_all, first, head_block, 1)
            cache_scores = jnp.einsum('ihc,tc->hit', query_part, latent32, precision=highest) + jnp.einsum('ihe,te->hit', rope_part, rope32, precision=highest)
            cache_scores = jnp.where(in_cache[None, None, :], cache_scores * score_scale, masked_value)
            tree_scores = jnp.einsum('ihc,jc->hij', query_part, draft32, precision=highest) + jnp.einsum('ihe,je->hij', rope_part, draft_rope32, precision=highest)
            tree_scores = jnp.where(ancestors[None, :, :], tree_scores * score_scale, masked_value)
            row_top = jnp.maximum(lax.optimization_barrier(jnp.max(cache_scores, axis=2)), lax.optimization_barrier(jnp.max(tree_scores, axis=2)))
            cache_weights = jnp.exp(cache_scores - row_top[:, :, None])
            tree_weights = jnp.exp(tree_scores - row_top[:, :, None])
            weight_total = lax.optimization_barrier(jnp.sum(cache_weights, axis=2)) + lax.optimization_barrier(jnp.sum(tree_weights, axis=2))
            latent_sum = jnp.einsum('hit,tc->hic', rounded(cache_weights), latent32, precision=highest) + jnp.einsum('hij,jc->hic', rounded(tree_weights), draft32, precision=highest)
            value_part = lax.dynamic_slice_in_dim(absorb_v32, first, head_block, 0)
            projected = jnp.einsum('hic,hcn->hin', latent_sum, value_part, precision=highest)
            return (projected / weight_total[:, :, None]).astype(jnp.bfloat16)
        blocks = lax.map(per_block, jnp.arange(H // head_block, dtype=jnp.int32))
        return jnp.transpose(blocks.reshape(H, DRAFT, HN), (1, 0, 2)).reshape(DRAFT, H * HN)
    head_rows = lax.map(one_request, (q_nope, q_rope, cache_latent, cache_rope, draft_latent, draft_rope, cache_len, ancestry))
    head_rows = head_rows.reshape(TOKENS, H * HN)
    stream = residual.astype(jnp.float32) + jnp.dot(head_rows, out_proj, preferred_element_type=jnp.float32)
    hidden_out = stream.astype(jnp.bfloat16)
    mean_square = lax.optimization_barrier(jnp.mean(stream * stream, axis=1, keepdims=True))
    normed = (stream * lax.rsqrt(mean_square + norm_epsilon) * norm_gain).astype(jnp.bfloat16)
    logits = jnp.dot(normed, lm_head.T, preferred_element_type=jnp.float32)
    row_top = lax.optimization_barrier(jnp.max(logits, axis=1))
    log_total = row_top + jnp.log(lax.optimization_barrier(jnp.sum(jnp.exp(logits - row_top[:, None]), axis=1)))
    parent_rows = (jnp.arange(REQUESTS, dtype=jnp.int32)[:, None] * DRAFT + parent).reshape(-1)
    chosen = logits[parent_rows, draft_ids.reshape(-1)]
    target_logp = (chosen - log_total[parent_rows]).reshape(REQUESTS, DRAFT)
    accepted_score = lax.optimization_barrier(jnp.sum(jnp.where(jnp.arange(DRAFT, dtype=jnp.int32)[None, :] < accept_len[:, None], target_logp, 0.0), axis=1))
    return (hidden_out, target_logp, accepted_score)
```

```python
import functools
import math

import jax
import jax.numpy as jnp
from jax import lax
from jax.sharding import Mesh
from jax.sharding import PartitionSpec as P

from jax.experimental import pallas as pl
from jax.experimental.pallas import tpu as pltpu


MESH_ID = pl.DeviceIdType.MESH
LOWEST = -1e28
MASKED = -1e30
TRANS_B = (((1,), (1,)), ((), ()))


def attention_kernel(scale, len_ref, q_ref, kl_ref, kr_ref, draft_ref, parent_ref, av_ref, out_ref,
                     qbuf, kbuf, krbuf, avbuf, acc, top, mass, part, part_in, stat, stat_in, lse,
                     loc_sem, q_send, q_recv, k_send, k_recv, r_send, r_recv, v_send, v_recv, p_send, p_recv):
    y, z, c = lax.axis_index("seq_0"), lax.axis_index("seq_1"), lax.axis_index("batch_1")
    turn = lambda at, by: lax.rem(at + by, 4)
    y_right, y_left, y_far = {"seq_0": turn(y, 1)}, {"seq_0": turn(y, 3)}, {"seq_0": turn(y, 2)}
    z_right, z_left = {"seq_1": turn(z, 1)}, {"seq_1": turn(z, 3)}
    sibling = {"batch_1": 1 - c}
    barrier = pltpu.get_barrier_semaphore()
    for peer in (y_right, y_left, y_far, z_right, z_left, sibling):
        pl.semaphore_signal(barrier, inc=1, device_id=peer, device_id_type=MESH_ID)
    local = [
        pltpu.make_async_copy(kl_ref.at[pl.ds(512 * h, 512)], kbuf.at[h, :, pl.ds(0, 512)], loc_sem.at[h])
        for h in range(2)
    ]
    for copy in local:
        copy.start()
    own_av = pltpu.make_async_copy(av_ref, avbuf.at[0], loc_sem.at[2])
    own_av.start()
    own_q = pltpu.make_async_copy(q_ref, qbuf.at[0], loc_sem.at[3])
    own_q.start()
    own_r = pltpu.make_async_copy(kr_ref, krbuf.at[pl.ds(0, 2)], loc_sem.at[4])
    own_r.start()
    pl.semaphore_wait(barrier, 6)

    def remote(src, dst, send, recv, peer):
        copy = pltpu.make_async_remote_copy(src_ref=src, dst_ref=dst, send_sem=send, recv_sem=recv,
                                            device_id=peer, device_id_type=MESH_ID)
        copy.start()
        return copy

    half = lambda h: pl.ds(256 * h, 256)
    sends = []
    q_in, k_in, r_in = {}, {}, {}
    for slot, peer, order in ((1, y_right, (0, 1)), (2, y_left, (1, 0))):
        for h in order:
            n = slot * 2 + h
            q_in[n] = remote(q_ref.at[half(h)], qbuf.at[slot, half(h)], q_send.at[n], q_recv.at[n], peer)
    for slot, peer, order in ((1, z_right, (0, 1)), (2, z_left, (1, 0))):
        for h in order:
            n = slot * 2 + h
            k_in[n] = remote(kl_ref.at[pl.ds(512 * h, 512)], kbuf.at[n, :, pl.ds(0, 512)], k_send.at[n], k_recv.at[n], peer)
            r_in[n] = remote(kr_ref.at[h], krbuf.at[n], r_send.at[n], r_recv.at[n], peer)

    acc[...] = jnp.zeros_like(acc)
    top[...] = jnp.full(top.shape, LOWEST, jnp.float32)
    mass[...] = jnp.zeros_like(mass)

    row = lax.broadcasted_iota(jnp.int32, (128, 128), 0)
    col = lax.broadcasted_iota(jnp.int32, (128, 128), 1)
    hop = ((parent_ref[...] == col) & (row > 0) & (row < 64)).astype(jnp.float32)
    known = (row == col).astype(jnp.float32)
    for _ in range(6):
        step = hop.astype(jnp.bfloat16)
        known = known + jnp.dot(known.astype(jnp.bfloat16), step, preferred_element_type=jnp.float32)
        hop = jnp.dot(step, step, preferred_element_type=jnp.float32)
    tree_bias = jnp.where((known > 0.5) & (col < 64), 0.0, MASKED)[:64]

    def update(slot, rows, count, keys, values, bias):
        width = bias.shape[1]
        at = (slot, pl.ds(rows, count))
        scores = lax.dot_general(qbuf[at], keys, TRANS_B, preferred_element_type=jnp.float32)
        scores = scores * scale + bias
        before = top[at]
        now = jnp.maximum(before, jnp.max(scores, axis=1, keepdims=True))
        weights = jnp.exp2(scores - jnp.tile(now, (1, width // 128)))
        fade = jnp.exp2(before - now)
        total = mass[at] * fade
        for k in range(width // 128):
            total = total + weights[:, 128 * k : 128 * k + 128]
        mass[at] = total
        top[at] = now
        acc[at] = acc[at] * jnp.tile(fade, (1, 4)) + jnp.dot(
            weights.astype(jnp.bfloat16), values, preferred_element_type=jnp.float32
        )

    own_q.wait()
    for h in range(8):
        update(0, 64 * h, 64, draft_ref[...], draft_ref[:, :512], tree_bias)

    ROWS = 256

    def chunks(first, count, slots_first, slots):
        def chunk(kc, _):
            source = lax.rem(z + jnp.where(kc // 2 == 0, 0, jnp.where(kc // 2 == 1, 3, jnp.where(kc // 2 == 2, 1, 2))), 4)
            start = (y * 4 + source) * 1024 + lax.rem(kc, 2) * 512
            spot = start + lax.broadcasted_iota(jnp.int32, (1, 512), 1)
            bias = jnp.where(spot < len_ref[0], 0.0, MASKED)

            def block(n, _):
                update(slots_first + n // (512 // ROWS), pl.multiple_of(lax.rem(n, 512 // ROWS) * ROWS, ROWS), ROWS,
                       kbuf[kc], kbuf[kc, :, :512], bias)
                return 0

            return lax.fori_loop(0, slots * (512 // ROWS), block, 0)

        lax.fori_loop(first, first + count, chunk, 0)

    def rope_in(n):
        packed = krbuf[n].astype(jnp.float32)
        kbuf[n, pl.ds(0, 256), pl.ds(512, 128)] = packed.astype(jnp.bfloat16)
        kbuf[n, pl.ds(256, 256), pl.ds(512, 128)] = pltpu.roll(packed, 64, 1).astype(jnp.bfloat16)

    for copy in local:
        copy.wait()
    own_r.wait()
    for n in range(2):
        rope_in(n)
    chunks(0, 2, 0, 1)

    q_in[2].wait_recv()
    q_in[6] = remote(qbuf.at[1, half(0)], qbuf.at[3, half(0)], q_send.at[6], q_recv.at[6], y_right)
    q_in[5].wait_recv()
    q_in[7] = remote(qbuf.at[2, half(1)], qbuf.at[3, half(1)], q_send.at[7], q_recv.at[7], y_left)
    q_in[3].wait_recv()
    q_in[4].wait_recv()
    chunks(0, 2, 1, 2)

    def key_wait(n):
        k_in[n].wait_recv()
        r_in[n].wait_recv()

    def key_on(n, m, peer):
        k_in[m] = remote(kbuf.at[n, :, pl.ds(0, 512)], kbuf.at[m, :, pl.ds(0, 512)], k_send.at[m], k_recv.at[m], peer)
        r_in[m] = remote(krbuf.at[n], krbuf.at[m], r_send.at[m], r_recv.at[m], peer)

    key_wait(2)
    key_on(2, 6, z_right)
    key_wait(5)
    key_on(5, 7, z_left)
    rope_in(2)
    rope_in(5)
    chunks(2, 1, 0, 3)
    chunks(5, 1, 0, 3)
    q_in[6].wait_recv()
    q_in[7].wait_recv()
    v_in = {}
    mine = 4 * c
    pair = lambda first, h: pl.ds(first + 2 * h, 2)
    for slot, peer, order in ((1, y_right, (0, 1)), (2, y_left, (1, 0))):
        for h in order:
            n = slot * 2 + h
            v_in[n] = remote(av_ref.at[pair(mine, h)], avbuf.at[slot, pair(mine, h)], v_send.at[n], v_recv.at[n], peer)
    chunks(0, 3, 3, 1)
    chunks(5, 1, 3, 1)
    v_in[2].wait_recv()
    v_in[6] = remote(avbuf.at[1, pair(mine, 0)], avbuf.at[3, pair(mine, 0)], v_send.at[6], v_recv.at[6], y_right)
    v_in[5].wait_recv()
    v_in[7] = remote(avbuf.at[2, pair(mine, 1)], avbuf.at[3, pair(mine, 1)], v_send.at[7], v_recv.at[7], y_left)
    key_wait(3)
    key_wait(4)
    rope_in(3)
    rope_in(4)
    chunks(3, 2, 0, 4)
    v_in[3].wait_recv()
    v_in[4].wait_recv()
    v_over = {}
    for slot in (1, 2):
        v_over[slot] = remote(avbuf.at[slot, pl.ds(mine, 4)], avbuf.at[slot, pl.ds(mine, 4)], v_send.at[7 + slot], v_recv.at[7 + slot], sibling)
    v_in[6].wait_recv()
    v_in[7].wait_recv()
    v_over[3] = remote(avbuf.at[3, pl.ds(mine, 4)], avbuf.at[3, pl.ds(mine, 4)], v_send.at[10], v_recv.at[10], sibling)
    key_wait(6)
    key_wait(7)
    rope_in(6)
    rope_in(7)
    chunks(6, 2, 0, 4)
    own_av.wait()
    for slot in (1, 2, 3):
        v_over[slot].wait_recv()

    def finish(slot):
        def head(h, _):
            at = (slot, pl.ds(pl.multiple_of(64 * h, 64), 64))
            total = jnp.sum(mass[at], axis=1, keepdims=True)
            some = total > 0.0
            safe = jnp.where(some, total, 1.0)
            value = jnp.dot(acc[at].astype(jnp.bfloat16), avbuf[slot, h], preferred_element_type=jnp.float32)
            part[at] = (value * jnp.where(some, 1.0 / safe, 0.0)).astype(jnp.bfloat16)
            lse[pl.ds(pl.multiple_of(64 * h, 64), 64)] = jnp.where(some, top[at] + jnp.log2(safe), LOWEST)
            return 0

        lax.fori_loop(0, 8, head, 0)
        for k in range(4):
            stat[slot, pl.ds(k, 1)] = jnp.transpose(lse[pl.ds(128 * k, 128)])[:1]

    p_in = []
    for slot, place, peer in ((3, 3, y_far), (1, 2, y_left), (2, 1, y_right)):
        finish(slot)
        p_in.append(remote(part.at[slot], part_in.at[place], p_send.at[place], p_recv.at[place], peer))
        p_in.append(remote(stat.at[slot], stat_in.at[place], p_send.at[place + 4], p_recv.at[place + 4], peer))
    finish(0)
    for copy in p_in:
        copy.wait_recv()
    levels = [stat[0, :4]] + [stat_in[k, :4] for k in (1, 2, 3)]
    best = jnp.maximum(jnp.maximum(levels[0], levels[1]), jnp.maximum(levels[2], levels[3]))
    shares = [jnp.exp2(level - best) for level in levels]
    whole = 1.0 / (shares[0] + shares[1] + shares[2] + shares[3])
    for k in range(4):
        rows = pl.ds(128 * k, 128)
        mixed = jnp.zeros((128, 128), jnp.float32)
        for j in range(4):
            share = jnp.transpose(jnp.broadcast_to((shares[j] * whole)[k : k + 1], (128, 128)))
            block = part[0, rows] if j == 0 else part_in[j, rows]
            mixed = mixed + share * block.astype(jnp.float32)
        mixed = mixed.astype(jnp.bfloat16)
        out_ref[:, pl.ds(256 * k, 128)] = mixed[:64]
        out_ref[:, pl.ds(256 * k + 128, 128)] = mixed[64:]
    for table in (q_in, k_in, r_in, v_in, v_over):
        for copy in table.values():
            copy.wait_send()
    for copy in p_in:
        copy.wait_send()


def attention(q, kl, kr, draft, parent_col, absorb_v, cache_len, scale):
    bf, f32 = jnp.bfloat16, jnp.float32
    vm, hbm = pl.BlockSpec(memory_space=pltpu.VMEM), pl.BlockSpec(memory_space=pl.ANY)
    dma = pltpu.SemaphoreType.DMA
    return pl.pallas_call(
        functools.partial(attention_kernel, scale * math.log2(math.e)),
        out_shape=jax.ShapeDtypeStruct((64, 1024), bf),
        in_specs=[pl.BlockSpec(memory_space=pltpu.SMEM), hbm, hbm, hbm, vm, vm, hbm],
        out_specs=vm,
        scratch_shapes=[
            pltpu.VMEM((4, 512, 640), bf),
            pltpu.VMEM((8, 512, 640), bf),
            pltpu.VMEM((8, 256, 128), bf),
            pltpu.VMEM((4, 8, 512, 128), bf),
            pltpu.VMEM((4, 512, 512), f32),
            pltpu.VMEM((4, 512, 128), f32),
            pltpu.VMEM((4, 512, 128), f32),
            pltpu.VMEM((4, 512, 128), bf),
            pltpu.VMEM((4, 512, 128), bf),
            pltpu.VMEM((4, 8, 128), f32),
            pltpu.VMEM((4, 8, 128), f32),
            pltpu.VMEM((512, 128), f32),
            dma((5,)), dma((8,)), dma((8,)), dma((8,)), dma((8,)), dma((8,)), dma((8,)),
            dma((11,)), dma((11,)), dma((8,)), dma((8,)),
        ],
        compiler_params=pltpu.CompilerParams(collective_id=1, has_side_effects=True, vmem_limit_bytes=40 << 20),
        cost_estimate=pl.CostEstimate(flops=20_000_000_000, bytes_accessed=20_000_000, transcendentals=8_500_000),
        name="attention",
    )(cache_len, q, kl, kr, draft, parent_col, absorb_v)


SEQ = ("seq_0", "seq_1")
BATCH = ("batch_0", "batch_1")
SEQ_BATCH = ("seq_0", "seq_1", "batch_0", "batch_1")


masked_value = -1e30
norm_epsilon = 1e-06
highest = lax.Precision.HIGHEST


def sent_together(arrays, axis, dim, along):
    ends, at = ([], 0)
    for a in arrays[:-1]:
        at += a.shape[along]
        ends.append(at)
    both = jnp.concatenate(arrays, axis=along)
    return tuple(jnp.split(lax.all_gather(both, axis, axis=dim, tiled=True), ends, axis=along))


def copy_for_each(array, axis):
    copies = jnp.broadcast_to(array, (lax.axis_size(axis), *array.shape))
    return lax.all_to_all(copies, axis, split_axis=0, concat_axis=0, tiled=True)


def over_copies(array, axis):
    everything = copy_for_each(array, axis)
    return jnp.max(everything, axis=0)


def gathered_once(array, axis):
    leaves = jax.tree.leaves(array)
    sequence = sorted(range(len(leaves)), key=lambda k: -leaves[k].size)
    width = (1, *leaves[sequence[0]].shape)[-1]
    lines = [
        jnp.pad(leaves[k].reshape(-1), (0, -leaves[k].size % width)).reshape(-1, width)
        for k in sequence
    ]
    both, at, found = (lax.all_gather(jnp.concatenate(lines), axis), 0, {})
    for k, line in zip(sequence, lines):
        piece = both[:, at : at + len(line)].reshape(len(both), -1)
        found[k] = piece[:, : leaves[k].size].reshape(-1, *leaves[k].shape)
        at += len(line)
    numbers = iter(range(len(leaves)))
    return jax.tree.map(lambda _: found[next(numbers)], array)


def combined_by_axis(array, axes, combine):
    for axis in axes:
        pieces = gathered_once(array, axis)
        array = jax.tree.map(lambda part: part[0], pieces)
        for k in range(1, lax.axis_size(axis)):
            array = combine(array, jax.tree.map(lambda part: part[k], pieces))
    return array


def ancestry_of(parents):
    draft_count = parents.shape[1]
    indices = jnp.arange(draft_count, dtype=jnp.int32)
    parent_map = (
        (parents[:, :, None] == indices[None, None, :]) & (indices[None, :, None] > 0)
    ).astype(jnp.float32)
    ancestry = jnp.broadcast_to(jnp.eye(draft_count, dtype=jnp.float32), parent_map.shape)
    for doubling in range(draft_count.bit_length() - 1):
        ancestry = ancestry + jnp.einsum("rij,rjk->rik", ancestry, parent_map, precision=highest)
        parent_map = jnp.einsum("rij,rjk->rik", parent_map, parent_map, precision=highest)
    return ancestry > 0.5


def combine_soft(earlier, later):
    top_new = jnp.maximum(earlier[0], later[0])
    mass_new = earlier[1] * jnp.exp(earlier[0] - top_new) + later[1] * jnp.exp(later[0] - top_new)
    return (top_new, mass_new, earlier[2] + later[2])


def body(
    q_nope,
    q_rope,
    absorb_k,
    absorb_v,
    cache_latent,
    cache_rope,
    draft_latent,
    draft_rope,
    residual,
    out_proj,
    norm_gain,
    lm_head,
    parent,
    draft_ids,
    cache_len,
    accept_len,
):
    requests, draft_count, local_heads, nope_width = q_nope.shape
    score_scale = 1.0 / math.sqrt(nope_width + q_rope.shape[3])
    seq_index = lax.axis_index(SEQ)
    batch_index = lax.axis_index(BATCH)
    bf = jnp.bfloat16
    latent = jnp.einsum("ihn,hnc->hic", q_nope[0], absorb_k, preferred_element_type=jnp.float32)
    rope = jnp.pad(jnp.transpose(q_rope[0], (1, 0, 2)), ((0, 0), (0, 0), (0, 64)))
    query = jnp.concatenate([latent.astype(bf), rope], axis=2).reshape(512, 640)
    kr = cache_rope[0].reshape(2, 2, 256, 64).transpose(0, 2, 1, 3).reshape(2, 256, 128)
    draft = jnp.pad(jnp.concatenate([draft_latent[0], draft_rope[0]], axis=1), ((0, 64), (0, 64)))
    own_parent = lax.dynamic_slice_in_dim(parent, batch_index, 1, 0)[0]
    parent_col = jnp.broadcast_to(jnp.pad(own_parent, (0, 64))[:, None], (128, 128))
    head_rows = attention(query, cache_latent[0], kr, draft, parent_col, absorb_v, cache_len, score_scale)
    branch_term = jnp.dot(head_rows, out_proj, preferred_element_type=jnp.float32)
    width_local = residual.shape[1]
    feature_first = seq_index * width_local
    residual_wide = lax.dynamic_update_slice_in_dim(
        jnp.zeros_like(branch_term), residual.astype(jnp.float32), feature_first, 1
    )
    stream = lax.psum(branch_term + residual_wide, SEQ)
    square = jnp.sum(stream * stream, axis=1)
    normed = (
        stream * lax.rsqrt(square / stream.shape[1] + norm_epsilon)[:, None] * norm_gain
    ).astype(jnp.bfloat16)
    hidden_out = lax.dynamic_slice_in_dim(stream, feature_first, width_local, 1).astype(
        jnp.bfloat16
    )
    vocab_rows = lm_head.shape[0]
    vocab_first = lax.axis_index(SEQ_BATCH) * vocab_rows
    logits = jnp.einsum(
        "rd,vd->rv",
        lax.all_gather(normed, BATCH, axis=0, tiled=True),
        lm_head,
        preferred_element_type=jnp.float32,
    )
    request_total = parent.shape[0]
    parent_rows = (
        jnp.arange(request_total, dtype=jnp.int32)[:, None] * draft_count + parent
    ).reshape(-1)
    source = logits[parent_rows]
    column = jnp.arange(vocab_rows, dtype=jnp.int32) + vocab_first
    picked = jnp.sum(
        jnp.where(column[None, :] == draft_ids.reshape(-1)[:, None], source, 0.0), axis=1
    )
    local_best = jnp.max(logits, axis=1)
    local_mass = jnp.sum(jnp.exp(logits - local_best[:, None]), axis=1)
    best, exp_mass, chosen = combined_by_axis(
        (local_best, local_mass, picked), SEQ_BATCH, combine_soft
    )
    log_total = best + jnp.log(exp_mass)
    target_all = (chosen - log_total[parent_rows]).reshape(request_total, draft_count)
    target_logp = lax.dynamic_slice_in_dim(target_all, batch_index * requests, requests, 0)
    accepted_score = jnp.sum(
        jnp.where(
            jnp.arange(draft_count, dtype=jnp.int32)[None, :] < accept_len[:, None],
            target_logp,
            0.0,
        ),
        axis=1,
    )
    return (hidden_out, target_logp, accepted_score)


def solution(mesh):
    split = Mesh(mesh.devices.reshape(4, 4, 4, 2), ("seq_0", "seq_1", "batch_0", "batch_1"))
    in_specs = (
        P(BATCH, None, SEQ, None),
        P(BATCH, None, SEQ, None),
        P(SEQ, None, None),
        P(SEQ, None, None),
        P(BATCH, SEQ, None),
        P(BATCH, SEQ, None),
        P(BATCH, None, None),
        P(BATCH, None, None),
        P(BATCH, SEQ),
        P(SEQ, None),
        P(),
        P(SEQ_BATCH, None),
        P(),
        P(),
        P(BATCH),
        P(BATCH),
    )
    out_specs = (P(BATCH, SEQ), P(BATCH, None), P(BATCH))
    return jax.shard_map(body, mesh=split, in_specs=in_specs, out_specs=out_specs, check_vma=False)
```

```python
import functools
import math

import jax
import jax.numpy as jnp
from jax import lax
from jax.experimental import pallas as pl
from jax.experimental.pallas import tpu as pltpu
from jax.sharding import Mesh
from jax.sharding import PartitionSpec as P

SEQ = ("seq_0", "seq_1")
BATCH = ("batch_0", "batch_1")
SEQ_BATCH = ("seq_0", "seq_1", "batch_0", "batch_1")

norm_epsilon = 1e-06

MESH_ID = pl.DeviceIdType.MESH
LOWEST = -1e28
MASKED = -1e30
TRANS_B = (((1,), (1,)), ((), ()))


def attention_kernel(scale, len_ref, q_ref, kl_ref, kr_ref, draft_ref, parent_ref, av_ref, out_ref,
                     qbuf, kbuf, krbuf, avbuf, acc, top, mass, part, part_in, stat, stat_in, lse,
                     loc_sem, q_send, q_recv, k_send, k_recv, r_send, r_recv, v_send, v_recv, p_send, p_recv):
    y, z, c = lax.axis_index("seq_0"), lax.axis_index("seq_1"), lax.axis_index("batch_1")
    turn = lambda at, by: lax.rem(at + by, 4)
    y_right, y_left, y_far = {"seq_0": turn(y, 1)}, {"seq_0": turn(y, 3)}, {"seq_0": turn(y, 2)}
    z_right, z_left = {"seq_1": turn(z, 1)}, {"seq_1": turn(z, 3)}
    sibling = {"batch_1": 1 - c}
    barrier = pltpu.get_barrier_semaphore()
    for peer in (y_right, y_left, y_far, z_right, z_left, sibling):
        pl.semaphore_signal(barrier, inc=1, device_id=peer, device_id_type=MESH_ID)
    local = [
        pltpu.make_async_copy(kl_ref.at[pl.ds(512 * h, 512)], kbuf.at[h, :, pl.ds(0, 512)], loc_sem.at[h])
        for h in range(2)
    ]
    for copy in local:
        copy.start()
    own_av = pltpu.make_async_copy(av_ref, avbuf.at[0], loc_sem.at[2])
    own_av.start()
    own_q = pltpu.make_async_copy(q_ref, qbuf.at[0], loc_sem.at[3])
    own_q.start()
    own_r = pltpu.make_async_copy(kr_ref, krbuf.at[pl.ds(0, 2)], loc_sem.at[4])
    own_r.start()
    pl.semaphore_wait(barrier, 6)

    def remote(src, dst, send, recv, peer):
        copy = pltpu.make_async_remote_copy(src_ref=src, dst_ref=dst, send_sem=send, recv_sem=recv,
                                            device_id=peer, device_id_type=MESH_ID)
        copy.start()
        return copy

    half = lambda h: pl.ds(256 * h, 256)
    sends = []
    q_in, k_in, r_in = {}, {}, {}
    for slot, peer, order in ((1, y_right, (0, 1)), (2, y_left, (1, 0))):
        for h in order:
            n = slot * 2 + h
            q_in[n] = remote(q_ref.at[half(h)], qbuf.at[slot, half(h)], q_send.at[n], q_recv.at[n], peer)
    for slot, peer, order in ((1, z_right, (0, 1)), (2, z_left, (1, 0))):
        for h in order:
            n = slot * 2 + h
            k_in[n] = remote(kl_ref.at[pl.ds(512 * h, 512)], kbuf.at[n, :, pl.ds(0, 512)], k_send.at[n], k_recv.at[n], peer)
            r_in[n] = remote(kr_ref.at[h], krbuf.at[n], r_send.at[n], r_recv.at[n], peer)

    acc[...] = jnp.zeros_like(acc)
    top[...] = jnp.full(top.shape, LOWEST, jnp.float32)
    mass[...] = jnp.zeros_like(mass)

    row = lax.broadcasted_iota(jnp.int32, (128, 128), 0)
    col = lax.broadcasted_iota(jnp.int32, (128, 128), 1)
    hop = ((parent_ref[...] == col) & (row > 0) & (row < 64)).astype(jnp.float32)
    known = (row == col).astype(jnp.float32)
    for _ in range(6):
        step = hop.astype(jnp.bfloat16)
        known = known + jnp.dot(known.astype(jnp.bfloat16), step, preferred_element_type=jnp.float32)
        hop = jnp.dot(step, step, preferred_element_type=jnp.float32)
    tree_bias = jnp.where((known > 0.5) & (col < 64), 0.0, MASKED)[:64]

    def update(slot, rows, count, keys, values, bias):
        width = bias.shape[1]
        at = (slot, pl.ds(rows, count))
        scores = lax.dot_general(qbuf[at], keys, TRANS_B, preferred_element_type=jnp.float32)
        scores = scores * scale + bias
        before = top[at]
        now = jnp.maximum(before, jnp.max(scores, axis=1, keepdims=True))
        weights = jnp.exp2(scores - jnp.tile(now, (1, width // 128)))
        fade = jnp.exp2(before - now)
        total = mass[at] * fade
        for k in range(width // 128):
            total = total + weights[:, 128 * k : 128 * k + 128]
        mass[at] = total
        top[at] = now
        acc[at] = acc[at] * jnp.tile(fade, (1, 4)) + jnp.dot(
            weights.astype(jnp.bfloat16), values, preferred_element_type=jnp.float32
        )

    own_q.wait()
    for h in range(8):
        update(0, 64 * h, 64, draft_ref[...], draft_ref[:, :512], tree_bias)

    ROWS = 256

    def chunks(first, count, slots_first, slots):
        def chunk(kc, _):
            source = lax.rem(z + jnp.where(kc // 2 == 0, 0, jnp.where(kc // 2 == 1, 3, jnp.where(kc // 2 == 2, 1, 2))), 4)
            start = (y * 4 + source) * 1024 + lax.rem(kc, 2) * 512
            spot = start + lax.broadcasted_iota(jnp.int32, (1, 512), 1)
            bias = jnp.where(spot < len_ref[0], 0.0, MASKED)

            def block(n, _):
                update(slots_first + n // (512 // ROWS), pl.multiple_of(lax.rem(n, 512 // ROWS) * ROWS, ROWS), ROWS,
                       kbuf[kc], kbuf[kc, :, :512], bias)
                return 0

            return lax.fori_loop(0, slots * (512 // ROWS), block, 0)

        lax.fori_loop(first, first + count, chunk, 0)

    def rope_in(n):
        packed = krbuf[n].astype(jnp.float32)
        kbuf[n, pl.ds(0, 256), pl.ds(512, 128)] = packed.astype(jnp.bfloat16)
        kbuf[n, pl.ds(256, 256), pl.ds(512, 128)] = pltpu.roll(packed, 64, 1).astype(jnp.bfloat16)

    for copy in local:
        copy.wait()
    own_r.wait()
    for n in range(2):
        rope_in(n)
    chunks(0, 2, 0, 1)

    q_in[2].wait_recv()
    q_in[6] = remote(qbuf.at[1, half(0)], qbuf.at[3, half(0)], q_send.at[6], q_recv.at[6], y_right)
    q_in[5].wait_recv()
    q_in[7] = remote(qbuf.at[2, half(1)], qbuf.at[3, half(1)], q_send.at[7], q_recv.at[7], y_left)
    q_in[3].wait_recv()
    q_in[4].wait_recv()
    chunks(0, 2, 1, 2)

    def key_wait(n):
        k_in[n].wait_recv()
        r_in[n].wait_recv()

    def key_on(n, m, peer):
        k_in[m] = remote(kbuf.at[n, :, pl.ds(0, 512)], kbuf.at[m, :, pl.ds(0, 512)], k_send.at[m], k_recv.at[m], peer)
        r_in[m] = remote(krbuf.at[n], krbuf.at[m], r_send.at[m], r_recv.at[m], peer)

    key_wait(2)
    key_on(2, 6, z_right)
    key_wait(5)
    key_on(5, 7, z_left)
    rope_in(2)
    rope_in(5)
    chunks(2, 1, 0, 3)
    chunks(5, 1, 0, 3)
    q_in[6].wait_recv()
    q_in[7].wait_recv()
    v_in = {}
    mine = 4 * c
    pair = lambda first, h: pl.ds(first + 2 * h, 2)
    for slot, peer, order in ((1, y_right, (0, 1)), (2, y_left, (1, 0))):
        for h in order:
            n = slot * 2 + h
            v_in[n] = remote(av_ref.at[pair(mine, h)], avbuf.at[slot, pair(mine, h)], v_send.at[n], v_recv.at[n], peer)
    chunks(0, 3, 3, 1)
    chunks(5, 1, 3, 1)
    v_in[2].wait_recv()
    v_in[6] = remote(avbuf.at[1, pair(mine, 0)], avbuf.at[3, pair(mine, 0)], v_send.at[6], v_recv.at[6], y_right)
    v_in[5].wait_recv()
    v_in[7] = remote(avbuf.at[2, pair(mine, 1)], avbuf.at[3, pair(mine, 1)], v_send.at[7], v_recv.at[7], y_left)
    key_wait(3)
    key_wait(4)
    rope_in(3)
    rope_in(4)
    chunks(3, 2, 0, 4)
    v_in[3].wait_recv()
    v_in[4].wait_recv()
    v_over = {}
    for slot in (1, 2):
        v_over[slot] = remote(avbuf.at[slot, pl.ds(mine, 4)], avbuf.at[slot, pl.ds(mine, 4)], v_send.at[7 + slot], v_recv.at[7 + slot], sibling)
    v_in[6].wait_recv()
    v_in[7].wait_recv()
    v_over[3] = remote(avbuf.at[3, pl.ds(mine, 4)], avbuf.at[3, pl.ds(mine, 4)], v_send.at[10], v_recv.at[10], sibling)
    key_wait(6)
    key_wait(7)
    rope_in(6)
    rope_in(7)
    chunks(6, 2, 0, 4)
    own_av.wait()
    for slot in (1, 2, 3):
        v_over[slot].wait_recv()

    def finish(slot):
        def head(h, _):
            at = (slot, pl.ds(pl.multiple_of(64 * h, 64), 64))
            total = jnp.sum(mass[at], axis=1, keepdims=True)
            some = total > 0.0
            safe = jnp.where(some, total, 1.0)
            value = jnp.dot(acc[at].astype(jnp.bfloat16), avbuf[slot, h], preferred_element_type=jnp.float32)
            part[at] = (value * jnp.where(some, 1.0 / safe, 0.0)).astype(jnp.bfloat16)
            lse[pl.ds(pl.multiple_of(64 * h, 64), 64)] = jnp.where(some, top[at] + jnp.log2(safe), LOWEST)
            return 0

        lax.fori_loop(0, 8, head, 0)
        for k in range(4):
            stat[slot, pl.ds(k, 1)] = jnp.transpose(lse[pl.ds(128 * k, 128)])[:1]

    p_in = []
    for slot, place, peer in ((3, 3, y_far), (1, 2, y_left), (2, 1, y_right)):
        finish(slot)
        p_in.append(remote(part.at[slot], part_in.at[place], p_send.at[place], p_recv.at[place], peer))
        p_in.append(remote(stat.at[slot], stat_in.at[place], p_send.at[place + 4], p_recv.at[place + 4], peer))
    finish(0)
    for copy in p_in:
        copy.wait_recv()
    levels = [stat[0, :4]] + [stat_in[k, :4] for k in (1, 2, 3)]
    best = jnp.maximum(jnp.maximum(levels[0], levels[1]), jnp.maximum(levels[2], levels[3]))
    shares = [jnp.exp2(level - best) for level in levels]
    whole = 1.0 / (shares[0] + shares[1] + shares[2] + shares[3])
    for k in range(4):
        rows = pl.ds(128 * k, 128)
        mixed = jnp.zeros((128, 128), jnp.float32)
        for j in range(4):
            share = jnp.transpose(jnp.broadcast_to((shares[j] * whole)[k : k + 1], (128, 128)))
            block = part[0, rows] if j == 0 else part_in[j, rows]
            mixed = mixed + share * block.astype(jnp.float32)
        mixed = mixed.astype(jnp.bfloat16)
        out_ref[:, pl.ds(256 * k, 128)] = mixed[:64]
        out_ref[:, pl.ds(256 * k + 128, 128)] = mixed[64:]
    for table in (q_in, k_in, r_in, v_in, v_over):
        for copy in table.values():
            copy.wait_send()
    for copy in p_in:
        copy.wait_send()


def attention(q, kl, kr, draft, parent_col, absorb_v, cache_len, scale):
    bf, f32 = jnp.bfloat16, jnp.float32
    vm, hbm = pl.BlockSpec(memory_space=pltpu.VMEM), pl.BlockSpec(memory_space=pl.ANY)
    dma = pltpu.SemaphoreType.DMA
    return pl.pallas_call(
        functools.partial(attention_kernel, scale * math.log2(math.e)),
        out_shape=jax.ShapeDtypeStruct((64, 1024), bf),
        in_specs=[pl.BlockSpec(memory_space=pltpu.SMEM), hbm, hbm, hbm, vm, vm, hbm],
        out_specs=vm,
        scratch_shapes=[
            pltpu.VMEM((4, 512, 640), bf),
            pltpu.VMEM((8, 512, 640), bf),
            pltpu.VMEM((8, 256, 128), bf),
            pltpu.VMEM((4, 8, 512, 128), bf),
            pltpu.VMEM((4, 512, 512), f32),
            pltpu.VMEM((4, 512, 128), f32),
            pltpu.VMEM((4, 512, 128), f32),
            pltpu.VMEM((4, 512, 128), bf),
            pltpu.VMEM((4, 512, 128), bf),
            pltpu.VMEM((4, 8, 128), f32),
            pltpu.VMEM((4, 8, 128), f32),
            pltpu.VMEM((512, 128), f32),
            dma((5,)), dma((8,)), dma((8,)), dma((8,)), dma((8,)), dma((8,)), dma((8,)),
            dma((11,)), dma((11,)), dma((8,)), dma((8,)),
        ],
        compiler_params=pltpu.CompilerParams(collective_id=1, has_side_effects=True, vmem_limit_bytes=40 << 20),
        cost_estimate=pl.CostEstimate(flops=20_000_000_000, bytes_accessed=20_000_000, transcendentals=8_500_000),
        name="attention",
    )(cache_len, q, kl, kr, draft, parent_col, absorb_v)


def head_kernel(rows_ref, proj_ref, resid_ref, gain_ref, lm_ref, table_ref, accept_ref,
                hid_ref, target_ref, score_ref,
                part, part_in, near, near_in, hid_own, wide, lm, logits, tile, tile1, tile2,
                lm_sem, s_send, s_recv, n_sem, h_sem, g1_send, g1_recv, g2_send, g2_recv, g3_send, g3_recv,
                c_send, c_recv, f1_send, f1_recv, f2_send, f2_recv):
    y, z = lax.axis_index("seq_0"), lax.axis_index("seq_1")
    x, c = lax.axis_index("batch_0"), lax.axis_index("batch_1")
    zh, zl = z // 2, lax.rem(z, 2)
    me, group, place = y * 4 + z, y * 2 + z // 2, x * 2 + c
    bf, f32 = jnp.bfloat16, jnp.float32
    lm_copy = pltpu.make_async_copy(lm_ref, lm, lm_sem)
    lm_copy.start()

    def seq_peer(s):
        return {"seq_0": s // 4, "seq_1": lax.rem(s, 4)}

    def batch_peer(b):
        return {"batch_0": b // 2, "batch_1": lax.rem(b, 2)}

    barrier = pltpu.get_barrier_semaphore()

    def greet_seq(k, _):
        pl.semaphore_signal(barrier, inc=1, device_id=seq_peer(lax.rem(me + k, 16)), device_id_type=MESH_ID)
        return 0

    def greet_batch(k, _):
        pl.semaphore_signal(barrier, inc=1, device_id=batch_peer(lax.rem(place + k, 8)), device_id_type=MESH_ID)
        return 0

    lax.fori_loop(1, 16, greet_seq, 0)
    lax.fori_loop(1, 8, greet_batch, 0)

    def describe(src, dst, send, recv, peer):
        return pltpu.make_async_remote_copy(src_ref=src, dst_ref=dst, send_sem=send, recv_sem=recv,
                                            device_id=peer, device_id_type=MESH_ID)

    def remote(*spec):
        copy = describe(*spec)
        copy.start()
        return copy

    def product(g):
        return jnp.dot(rows_ref[...], proj_ref[:, pl.ds(pl.multiple_of(g * 896, 128), 896)], preferred_element_type=f32)

    def outward(s):
        return describe(part.at[s], part_in.at[me], s_send.at[s], s_recv.at[me], seq_peer(s))

    def inward(s):
        return describe(part.at[s], part_in.at[s], s_send.at[s], s_recv.at[s], seq_peer(s))

    def make(g):
        block = product(g).astype(bf)
        part[2 * g] = block[:32]
        part[2 * g + 1] = block[32:]

    make(lax.rem(group + 1, 8))
    pl.semaphore_wait(barrier, 22)

    def spread(k, _):
        g = lax.rem(group + k, 8)
        outward(2 * g).start()
        outward(2 * g + 1).start()

        @pl.when(k < 7)
        def _():
            make(lax.rem(group + k + 1, 8))

        return 0

    lax.fori_loop(1, 8, spread, 0)
    mine = product(group) + resid_ref[...].astype(f32)
    first = zl == 0
    near[...] = jnp.where(first, mine[32:], mine[:32])
    partner = {"seq_1": zh * 2 + 1 - zl}
    near_copy = remote(near, near_in, n_sem.at[0], n_sem.at[1], partner)
    stream = jnp.where(first, mine[:32], mine[32:])
    other = group * 2

    def collect(k, total):
        s = lax.rem(other + 1 + k, 16)
        inward(s).wait_recv()
        return total + part_in[s].astype(f32)

    stream = lax.fori_loop(1, 15, collect, stream)
    near_copy.wait_recv()
    stream = stream + near_in[...]

    squares = jnp.sum(stream * stream, axis=1, keepdims=True)
    high = squares.astype(bf)
    low = (squares - high.astype(f32)).astype(bf)
    lane = lax.broadcasted_iota(jnp.int32, (32, 128), 1)
    at = (y, zh, x, c, zl)
    wide[(*at, slice(None), pl.ds(0, 896))] = (stream * gain_ref[:, pl.ds(pl.multiple_of(group * 896, 128), 896)]).astype(bf)
    wide[(*at, slice(None), pl.ds(896, 128))] = jnp.where(lane < 64, high.astype(f32), low.astype(f32)).astype(bf)

    lanes = (pl.ds(0, 384), pl.ds(384, 384), pl.ds(768, 256))
    every = slice(None)
    along = {"x": ("batch_0", x), "y": ("seq_0", y), "z": ("seq_1", z)}

    def turned(axis, by):
        name, own = along[axis]
        return {name: lax.rem(own + by, 4)}

    def view(p, done, pos, half=None):
        py, pz, px = pos["y"], pos["z"], pos["x"]
        iy = every if "y" in done else py
        izh, izl = (every, every) if "z" in done else (pz // 2, lax.rem(pz, 2))
        ix = every if "x" in done else px
        if half is not None:
            if "y" in done:
                iy = pl.ds(2 * half, 2)
            else:
                izh = pl.ds(half, 1)
        return wide.at[iy, izh, ix, pos.get("c", c), izl, :, lanes[p]]

    orders = (("x", "y", "z"), ("y", "z", "x"), ("z", "x", "y"))
    here = {"x": x, "y": y, "z": z}

    def moved(axis, by):
        return {**here, axis: lax.rem(here[axis] + by, 4)}

    pending = []
    hid_own[...] = stream.astype(bf)
    hid_copy = None
    waits = {}
    for stage, (sends, recvs) in enumerate(((g1_send, g1_recv), (g2_send, g2_recv))):
        for p in range(3):
            axis, done = orders[p][stage], orders[p][:stage]
            for k in (1, 3, 2):
                n = p * 3 + k - 1
                own = view(p, done, here)
                copy = remote(own, own, sends.at[n], recvs.at[n], turned(axis, k))
                pending.append(copy)
                waits[stage, p, k] = (done, axis, n, sends, recvs)
        if stage == 0:
            hid_copy = remote(hid_own, hid_ref.at[zl], h_sem.at[0], h_sem.at[1], partner)
            hid_ref[zl] = hid_own[...]
        for p in range(3):
            done, axis = orders[p][:stage], orders[p][stage]
            for k in (1, 3, 2):
                n = p * 3 + k - 1
                came = view(p, done, moved(axis, 4 - k))
                describe(came, came, sends.at[n], recvs.at[n], turned(axis, k)).wait_recv()
    sibling = {"batch_1": 1 - c}

    def over(p, n, which):
        copy = remote(which, which, c_send.at[n], c_recv.at[n], sibling)
        pending.append(copy)

    for p in range(3):
        axis, done = orders[p][2], orders[p][:2]
        for k, halves in ((1, (0, 1)), (3, (1, 0))):
            for half in halves:
                n = p * 6 + (k // 2) * 2 + half
                own = view(p, done, here, half)
                pending.append(remote(own, own, g3_send.at[n], g3_recv.at[n], turned(axis, k)))
    for p in range(3):
        over(p, p * 4, view(p, orders[p][:2], here))

    def came3(p, k, half):
        axis, done = orders[p][2], orders[p][:2]
        n = p * 6 + {1: 0, 3: 2, 2: 4}[k] + half
        block = view(p, done, moved(axis, 4 - k), half)
        describe(block, block, g3_send.at[n], g3_recv.at[n], turned(axis, 1)).wait_recv()
        return block

    def column(r):
        return jnp.transpose(jnp.broadcast_to(table_ref[pl.ds(r, 1)], (128, 128)))

    for p in range(3):
        axis = orders[p][2]
        block = came3(p, 1, 0)
        pending.append(remote(block, block, g3_send.at[p * 6 + 4], g3_recv.at[p * 6 + 4], turned(axis, 1)))
        block = came3(p, 3, 1)
        pending.append(remote(block, block, g3_send.at[p * 6 + 5], g3_recv.at[p * 6 + 5], turned(axis, 3)))
    for p in range(3):
        axis, done = orders[p][2], orders[p][:2]
        came3(p, 1, 1)
        over(p, p * 4 + 1, view(p, done, moved(axis, 3)))
        came3(p, 3, 0)
        over(p, p * 4 + 2, view(p, done, moved(axis, 1)))
    for p in range(3):
        axis, done = orders[p][2], orders[p][:2]
        came3(p, 2, 0)
        came3(p, 2, 1)
        over(p, p * 4 + 3, view(p, done, moved(axis, 2)))
    for p in range(3):
        axis, done = orders[p][2], orders[p][:2]
        for n, by in ((0, 0), (1, 3), (2, 1), (3, 2)):
            block = view(p, done, {**moved(axis, by), "c": 1 - c})
            describe(block, block, c_send.at[p * 4 + n], c_recv.at[p * 4 + n], sibling).wait_recv()
    lm_copy.wait()

    logits[...] = jnp.zeros_like(logits)
    tile[...] = jnp.zeros_like(tile)

    def contract(g, squares):
        left = wide[g // 2, lax.rem(g, 2)].reshape(512, 1024)
        right = lm[:, pl.ds(pl.multiple_of(g * 896, 128), 896)]
        logits[...] += lax.dot_general(left[:, :896], right, TRANS_B, preferred_element_type=f32)
        return squares + left[:, 896:].astype(f32)

    squares = lax.fori_loop(0, 8, contract, jnp.zeros((512, 128), f32))
    squares = jnp.sum(squares, axis=1, keepdims=True) * (1.0 / 64)
    rate = lax.rsqrt(squares * (1.0 / 7168) + norm_epsilon)
    vocab_first = (me * 8 + place) * 512
    entry = lax.broadcasted_iota(jnp.int32, (64, 512), 1) + vocab_first
    spot = lax.broadcasted_iota(jnp.int32, (64, 128), 1)
    for k in range(4):
        parents, wanted = column(k), column(4 + k)
        bests, masses, picks = [], [], []
        for h in range(2):
            rows = slice(128 * k + 64 * h, 128 * k + 64 * h + 64)
            values = logits[rows] * rate[rows]
            best = jnp.max(values, axis=1, keepdims=True)
            mass = jnp.sum(jnp.exp(values - best), axis=1, keepdims=True)
            choose = (parents[64 * h : 64 * h + 64].astype(jnp.int32) == spot).astype(bf)[:, :64]
            rest, source = values, jnp.zeros((64, 512), f32)
            for _ in range(3):
                piece = rest.astype(bf)
                source = source + jnp.dot(choose, piece, preferred_element_type=f32)
                rest = rest - piece.astype(f32)
            hit = entry == jnp.tile(wanted[64 * h : 64 * h + 64].astype(jnp.int32), (1, 4))
            pick = jnp.sum(jnp.where(hit, source, 0.0), axis=1, keepdims=True)
            for found, one in ((bests, best), (masses, mass), (picks, pick)):
                found.append(jnp.broadcast_to(one, (64, 128)))
        for i, found in enumerate((bests, masses, picks)):
            tile[pl.ds(4 * i + k, 1)] = jnp.transpose(jnp.concatenate(found, axis=0))[:1]

    def merge(blocks):
        best = functools.reduce(jnp.maximum, [b[0:4] for b in blocks])
        mass = sum(b[4:8] * jnp.exp(b[0:4] - best) for b in blocks)
        return best, mass, sum(b[8:12] for b in blocks)

    def exchange(landing, sends, recvs, count, own, peer):
        for k in range(1, count):
            pending.append(remote(tile, landing.at[k], sends.at[k], recvs.at[k], peer(lax.rem(own + k, count))))
        found = [tile[...]]
        for k in range(1, count):
            describe(tile, landing.at[k], sends.at[k], recvs.at[k], peer(lax.rem(own + k, count))).wait_recv()
            found.append(landing[k])
        for copy in pending[1 - count :]:
            copy.wait_send()
        del pending[1 - count :]
        return merge(found)

    best, mass, pick = exchange(tile1, f1_send, f1_recv, 8, place, batch_peer)
    tile[pl.ds(0, 4)] = best
    tile[pl.ds(4, 4)] = mass
    tile[pl.ds(8, 4)] = pick
    best, mass, pick = exchange(tile2, f2_send, f2_recv, 16, me, seq_peer)
    total = best + jnp.log(mass)

    def own_row(values):
        line = lax.broadcasted_iota(jnp.int32, (4, 128), 0)
        row = jnp.sum(jnp.where(line == x, values, 0.0), axis=0, keepdims=True)
        row = jnp.broadcast_to(row, (128, 128))
        return jnp.where(c == 0, row, pltpu.roll(row, 64, 1))

    lane = lax.broadcasted_iota(jnp.int32, (128, 128), 1)
    parents = jnp.transpose(own_row(table_ref[0:4])).astype(jnp.int32)
    of_parent = jnp.sum(jnp.where((parents == lane) & (lane < 64), own_row(total), 0.0), axis=1, keepdims=True)
    of_parent = jnp.transpose(jnp.broadcast_to(of_parent, (128, 128)))[:8]
    target = own_row(pick)[:8] - of_parent
    target_ref[...] = target
    kept = lane[:8] < jnp.minimum(accept_ref[0], 64)
    score_ref[...] = jnp.broadcast_to(jnp.sum(jnp.where(kept, target, 0.0), axis=1, keepdims=True), (8, 128))

    hid_back = describe(hid_own, hid_ref.at[1 - zl], h_sem.at[0], h_sem.at[1], partner)
    hid_back.wait_recv()
    hid_copy.wait_send()
    near_copy.wait_send()

    def sent(k, _):
        outward(lax.rem(other + 1 + k, 16)).wait_send()
        return 0

    lax.fori_loop(1, 15, sent, 0)
    for copy in pending:
        copy.wait_send()


def head(rows, proj, resid, gain, lm_head, table, accept):
    bf, f32 = jnp.bfloat16, jnp.float32
    vm, hbm = pl.BlockSpec(memory_space=pltpu.VMEM), pl.BlockSpec(memory_space=pl.ANY)
    dma = pltpu.SemaphoreType.DMA
    return pl.pallas_call(
        head_kernel,
        out_shape=(
            jax.ShapeDtypeStruct((2, 32, 896), bf),
            jax.ShapeDtypeStruct((8, 128), f32),
            jax.ShapeDtypeStruct((8, 128), f32),
        ),
        in_specs=[vm, vm, vm, vm, hbm, vm, pl.BlockSpec(memory_space=pltpu.SMEM)],
        out_specs=(vm, vm, vm),
        scratch_shapes=[
            pltpu.VMEM((16, 32, 896), bf),
            pltpu.VMEM((16, 32, 896), bf),
            pltpu.VMEM((32, 896), f32),
            pltpu.VMEM((32, 896), f32),
            pltpu.VMEM((32, 896), bf),
            pltpu.VMEM((4, 2, 4, 2, 2, 32, 1024), bf),
            pltpu.VMEM((512, 7168), bf),
            pltpu.VMEM((512, 512), f32),
            pltpu.VMEM((16, 128), f32),
            pltpu.VMEM((8, 16, 128), f32),
            pltpu.VMEM((16, 16, 128), f32),
            dma, dma((16,)), dma((16,)), dma((2,)), dma((2,)), dma((9,)), dma((9,)), dma((9,)), dma((9,)),
            dma((18,)), dma((18,)), dma((12,)), dma((12,)), dma((8,)), dma((8,)), dma((16,)), dma((16,)),
        ],
        compiler_params=pltpu.CompilerParams(collective_id=2, has_side_effects=True, vmem_limit_bytes=50 << 20),
        cost_estimate=pl.CostEstimate(flops=5_000_000_000, bytes_accessed=22_000_000, transcendentals=300_000),
        name="head",
    )(rows, proj, resid, gain, lm_head, table, accept)


def body(
    q_nope,
    q_rope,
    absorb_k,
    absorb_v,
    cache_latent,
    cache_rope,
    draft_latent,
    draft_rope,
    residual,
    out_proj,
    norm_gain,
    lm_head,
    parent,
    draft_ids,
    cache_len,
    accept_len,
):
    score_scale = 1.0 / math.sqrt(q_nope.shape[3] + q_rope.shape[3])
    batch_index = lax.axis_index(BATCH)
    bf = jnp.bfloat16
    latent = jnp.einsum("ihn,hnc->hic", q_nope[0], absorb_k, preferred_element_type=jnp.float32)
    rope = jnp.pad(jnp.transpose(q_rope[0], (1, 0, 2)), ((0, 0), (0, 0), (0, 64)))
    query = jnp.concatenate([latent.astype(bf), rope], axis=2).reshape(512, 640)
    kr = cache_rope[0].reshape(2, 2, 256, 64).transpose(0, 2, 1, 3).reshape(2, 256, 128)
    draft = jnp.pad(jnp.concatenate([draft_latent[0], draft_rope[0]], axis=1), ((0, 64), (0, 64)))
    own_parent = lax.dynamic_slice_in_dim(parent, batch_index, 1, 0)[0]
    parent_col = jnp.broadcast_to(jnp.pad(own_parent, (0, 64))[:, None], (128, 128))
    odd = lax.rem(lax.axis_index("seq_1"), 2) == 1
    resid = jnp.where(odd, jnp.pad(residual, ((0, 0), (448, 0))), jnp.pad(residual, ((0, 0), (0, 448))))
    table = jnp.concatenate([parent.reshape(4, 128), draft_ids.reshape(4, 128)], axis=0).astype(jnp.float32)
    head_rows = attention(query, cache_latent[0], kr, draft, parent_col, absorb_v, cache_len, score_scale)
    hidden, target, score = head(head_rows, out_proj, resid, norm_gain[None], lm_head, table, accept_len)
    hidden = hidden.reshape(64, 896)
    hidden_out = jnp.where(odd, hidden[:, 448:], hidden[:, :448])
    return (hidden_out, target[:1, :64], score[0, :1])


def solution(mesh):
    split = Mesh(mesh.devices.reshape(4, 4, 4, 2), ("seq_0", "seq_1", "batch_0", "batch_1"))
    in_specs = (
        P(BATCH, None, SEQ, None),
        P(BATCH, None, SEQ, None),
        P(SEQ, None, None),
        P(SEQ, None, None),
        P(BATCH, SEQ, None),
        P(BATCH, SEQ, None),
        P(BATCH, None, None),
        P(BATCH, None, None),
        P(BATCH, SEQ),
        P(SEQ, None),
        P(),
        P(SEQ_BATCH, None),
        P(),
        P(),
        P(BATCH),
        P(BATCH),
    )
    out_specs = (P(BATCH, SEQ), P(BATCH, None), P(BATCH))
    return jax.shard_map(body, mesh=split, in_specs=in_specs, out_specs=out_specs, check_vma=False)
```

```python
import functools
import math

import jax
import jax.numpy as jnp
from jax import lax
from jax.experimental import pallas as pl
from jax.experimental.pallas import tpu as pltpu
from jax.sharding import Mesh
from jax.sharding import PartitionSpec as P

SEQ = ("seq_0", "seq_1")
BATCH = ("batch_0", "batch_1")
SEQ_BATCH = ("seq_0", "seq_1", "batch_0", "batch_1")

norm_epsilon = 1e-06
MESH_ID = pl.DeviceIdType.MESH
LOWEST = -1e28
MASKED = -1e30
TRANS_B = (((1,), (1,)), ((), ()))


def whole_kernel(scale, len_ref, accept_ref, nope_ref, rope_ref, ak_ref, kl_ref, kr_ref, dl_ref, dr_ref, parent_ref, ids_ref,
                 av_ref, proj_ref, resid_ref, gain_ref, lm_ref, hid_ref, target_ref, score_ref,
                 qbuf, kbuf, krbuf, avbuf, acc, top, mass, part, part_in, stat, stat_in, lse, tree, names, rows_ref,
                 proj, lm, out_part, out_in, near, near_in, padded, hid_own, hid_in, wide, logits, rates, tiles, merged, tile1, tile2,
                 loc_sem, q_send, q_recv, k_send, k_recv, r_send, r_recv, v_send, v_recv, p_send, p_recv,
                 s_send, s_recv, n_sem, h_sem, g1_send, g1_recv, g2_send, g2_recv, g3_send, g3_recv,
                 c_send, c_recv, f1_send, f1_recv, f2_send, f2_recv):
    y, z = lax.axis_index("seq_0"), lax.axis_index("seq_1")
    x, c = lax.axis_index("batch_0"), lax.axis_index("batch_1")
    zh, zl = z // 2, lax.rem(z, 2)
    me, group, place = y * 4 + z, y * 2 + z // 2, x * 2 + c
    bf, f32 = jnp.bfloat16, jnp.float32
    turn = lambda at, by: lax.rem(at + by, 4)

    def seq_peer(s):
        return {"seq_0": s // 4, "seq_1": lax.rem(s, 4)}

    def batch_peer(b):
        return {"batch_0": b // 2, "batch_1": lax.rem(b, 2)}

    barrier = pltpu.get_barrier_semaphore()

    def greet_seq(k, _):
        pl.semaphore_signal(barrier, inc=1, device_id=seq_peer(lax.rem(me + k, 16)), device_id_type=MESH_ID)
        return 0

    def greet_batch(k, _):
        pl.semaphore_signal(barrier, inc=1, device_id=batch_peer(lax.rem(place + k, 8)), device_id_type=MESH_ID)
        return 0

    lax.fori_loop(1, 16, greet_seq, 0)
    lax.fori_loop(1, 8, greet_batch, 0)

    def describe(src, dst, send, recv, peer):
        return pltpu.make_async_remote_copy(src_ref=src, dst_ref=dst, send_sem=send, recv_sem=recv,
                                            device_id=peer, device_id_type=MESH_ID)

    def remote(*spec):
        copy = describe(*spec)
        copy.start()
        return copy

    def local_copy(src, dst, n):
        copy = pltpu.make_async_copy(src, dst, loc_sem.at[n])
        copy.start()
        return copy

    local = []
    for h in range(2):
        local.append(local_copy(kl_ref.at[pl.ds(512 * h, 512)], kbuf.at[h], h))
        local.append(local_copy(kr_ref.at[:, pl.ds(512 * h, 512)], krbuf.at[h, pl.ds(0, 64)], 2 + h))
    local_av = local_copy(av_ref, avbuf.at[0], 4)
    pl.semaphore_wait(barrier, 22)
    y_right, y_left, y_far = {"seq_0": turn(y, 1)}, {"seq_0": turn(y, 3)}, {"seq_0": turn(y, 2)}
    z_right, z_left = {"seq_1": turn(z, 1)}, {"seq_1": turn(z, 3)}
    sibling = {"batch_1": 1 - c}
    half = lambda h: pl.ds(256 * h, 256)
    sends = []
    q_in, k_in, r_in = {}, {}, {}
    for slot, peer, order in ((1, z_right, (0, 1)), (2, z_left, (1, 0))):
        for h in order:
            n = slot * 2 + h
            k_in[n] = remote(kl_ref.at[pl.ds(512 * h, 512)], kbuf.at[n], k_send.at[n], k_recv.at[n], peer)
            r_in[n] = remote(kr_ref.at[:, pl.ds(512 * h, 512)], krbuf.at[n, pl.ds(0, 64)], r_send.at[n], r_recv.at[n], peer)

    content = jnp.swapaxes(nope_ref[...].astype(f32), 0, 1).astype(bf)
    rotary = jnp.swapaxes(rope_ref[...].astype(f32), 0, 1).astype(bf)
    for h in range(8):
        rows = slice(64 * h, 64 * h + 64)
        qbuf[0, rows, 0:512] = jnp.dot(content[h], ak_ref[h], preferred_element_type=f32).astype(bf)
        qbuf[0, rows, 512:576] = rotary[h]
        qbuf[0, rows, 576:640] = jnp.zeros((64, 64), bf)
    for slot, peer, order in ((1, y_right, (0, 1)), (2, y_left, (1, 0))):
        for h in order:
            n = slot * 2 + h
            q_in[n] = remote(qbuf.at[0, half(h)], qbuf.at[slot, half(h)], q_send.at[n], q_recv.at[n], peer)
    proj_copy = local_copy(proj_ref, proj, 5)
    lm_copy = local_copy(lm_ref, lm, 6)
    acc[...] = jnp.zeros_like(acc)
    top[...] = jnp.full(top.shape, LOWEST, f32)
    mass[...] = jnp.zeros_like(mass)

    names[...] = jnp.zeros_like(names)
    names[0:8, 0:64] = parent_ref[...].astype(f32)
    names[8:16, 0:64] = ids_ref[...].astype(f32)
    own_line = lax.broadcasted_iota(jnp.int32, (8, 128), 0) == place
    own_parents = jnp.sum(jnp.where(own_line, names[0:8], 0.0), axis=0, keepdims=True)
    own_parents = jnp.transpose(jnp.broadcast_to(own_parents, (128, 128))).astype(jnp.int32)
    tree[...] = jnp.zeros_like(tree)
    tree[0:64, 0:512] = dl_ref[...]
    tree[0:64, 512:576] = dr_ref[...]
    for n in range(8):
        krbuf[n, 64:128] = jnp.zeros((64, 512), bf)
    row = lax.broadcasted_iota(jnp.int32, (128, 128), 0)
    col = lax.broadcasted_iota(jnp.int32, (128, 128), 1)
    hop = ((own_parents == col) & (row > 0) & (row < 64)).astype(f32)
    known = (row == col).astype(f32)
    for _ in range(6):
        step = hop.astype(bf)
        known = known + jnp.dot(known.astype(bf), step, preferred_element_type=f32)
        hop = jnp.dot(step, step, preferred_element_type=f32)
    tree_bias = jnp.where((known > 0.5) & (col < 64), 0.0, MASKED)[:64]

    def update(slot, rows, count, find, values, bias):
        width = bias.shape[1]
        at = (slot, pl.ds(rows, count))
        scores = find(qbuf[at]) * scale + bias
        before = top[at]
        now = jnp.maximum(before, jnp.max(scores, axis=1, keepdims=True))
        weights = jnp.exp2(scores - jnp.tile(now, (1, width // 128)))
        fade = jnp.exp2(before - now)
        total = mass[at] * fade
        for k in range(width // 128):
            total = total + weights[:, 128 * k : 128 * k + 128]
        mass[at] = total
        top[at] = now
        acc[at] = acc[at] * jnp.tile(fade, (1, 4)) + jnp.dot(
            weights.astype(bf), values, preferred_element_type=f32
        )

    def tree_scores(query):
        return lax.dot_general(query, tree[...], TRANS_B, preferred_element_type=f32)

    for h in range(8):
        update(0, 64 * h, 64, tree_scores, tree[:, :512], tree_bias)

    def chunks(first, count, slots):
        def chunk(kc, _):
            turn_by = jnp.where(kc // 2 == 0, 0, jnp.where(kc // 2 == 1, 3, jnp.where(kc // 2 == 2, 1, 2)))
            start = (y * 4 + lax.rem(z + turn_by, 4)) * 1024 + lax.rem(kc, 2) * 512
            spot = start + lax.broadcasted_iota(jnp.int32, (1, 512), 1)
            bias = jnp.where(spot < len_ref[0], 0.0, MASKED)
            def cache_scores(query):
                return lax.dot_general(query[:, :512], kbuf[kc], TRANS_B, preferred_element_type=f32) + jnp.dot(
                    query[:, 512:], krbuf[kc], preferred_element_type=f32
                )

            for slot in slots:
                update(slot, 0, 512, cache_scores, kbuf[kc], bias)
            return 0

        lax.fori_loop(first, first + count, chunk, 0)

    for copy in local:
        copy.wait()
    chunks(0, 2, (0,))

    q_in[2].wait_recv()
    q_in[6] = remote(qbuf.at[1, half(0)], qbuf.at[3, half(0)], q_send.at[6], q_recv.at[6], y_right)
    q_in[5].wait_recv()
    q_in[7] = remote(qbuf.at[2, half(1)], qbuf.at[3, half(1)], q_send.at[7], q_recv.at[7], y_left)
    q_in[3].wait_recv()
    q_in[4].wait_recv()
    chunks(0, 2, (1, 2))

    def key_wait(n):
        k_in[n].wait_recv()
        r_in[n].wait_recv()

    def key_on(n, m, peer):
        k_in[m] = remote(kbuf.at[n], kbuf.at[m], k_send.at[m], k_recv.at[m], peer)
        r_in[m] = remote(krbuf.at[n, pl.ds(0, 64)], krbuf.at[m, pl.ds(0, 64)], r_send.at[m], r_recv.at[m], peer)

    key_wait(2)
    key_on(2, 6, z_right)
    key_wait(5)
    key_on(5, 7, z_left)
    chunks(2, 1, (0, 1, 2))
    chunks(5, 1, (0, 1, 2))
    q_in[6].wait_recv()
    q_in[7].wait_recv()
    v_in = {}
    mine = 4 * c
    pair = lambda first, h: pl.ds(first + 2 * h, 2)
    for slot, peer, order in ((1, y_right, (0, 1)), (2, y_left, (1, 0))):
        for h in order:
            n = slot * 2 + h
            v_in[n] = remote(av_ref.at[pair(mine, h)], avbuf.at[slot, pair(mine, h)], v_send.at[n], v_recv.at[n], peer)
    chunks(0, 3, (3,))
    chunks(5, 1, (3,))
    v_in[2].wait_recv()
    v_in[6] = remote(avbuf.at[1, pair(mine, 0)], avbuf.at[3, pair(mine, 0)], v_send.at[6], v_recv.at[6], y_right)
    v_in[5].wait_recv()
    v_in[7] = remote(avbuf.at[2, pair(mine, 1)], avbuf.at[3, pair(mine, 1)], v_send.at[7], v_recv.at[7], y_left)
    key_wait(3)
    key_wait(4)
    chunks(3, 2, (0, 1, 2, 3))
    v_in[3].wait_recv()
    v_in[4].wait_recv()
    v_over = {}
    for slot in (1, 2):
        v_over[slot] = remote(avbuf.at[slot, pl.ds(mine, 4)], avbuf.at[slot, pl.ds(mine, 4)], v_send.at[7 + slot], v_recv.at[7 + slot], sibling)
    v_in[6].wait_recv()
    v_in[7].wait_recv()
    v_over[3] = remote(avbuf.at[3, pl.ds(mine, 4)], avbuf.at[3, pl.ds(mine, 4)], v_send.at[10], v_recv.at[10], sibling)
    key_wait(6)
    key_wait(7)
    local_av.wait()
    for slot in (1, 2, 3):
        v_over[slot].wait_recv()

    def finish(slot):
        for h in range(8):
            at = (slot, slice(64 * h, 64 * h + 64))
            total = jnp.sum(mass[at], axis=1, keepdims=True)
            some = total > 0.0
            safe = jnp.where(some, total, 1.0)
            value = jnp.dot(acc[at].astype(bf), avbuf[slot, h], preferred_element_type=f32)
            part[at] = (value * jnp.where(some, 1.0 / safe, 0.0)).astype(bf)
            lse[64 * h : 64 * h + 64] = jnp.where(some, top[at] + jnp.log2(safe), LOWEST)
        for k in range(4):
            stat[slot, pl.ds(k, 1)] = jnp.transpose(lse[pl.ds(128 * k, 128)])[:1]

    p_in = []
    for slot, landing, peer in ((3, 3, y_far), (1, 2, y_left), (2, 1, y_right)):
        chunks(6, 2, (slot,))
        finish(slot)
        p_in.append(remote(part.at[slot], part_in.at[landing], p_send.at[landing], p_recv.at[landing], peer))
        p_in.append(remote(stat.at[slot], stat_in.at[landing], p_send.at[landing + 4], p_recv.at[landing + 4], peer))
    chunks(6, 2, (0,))
    finish(0)
    for copy in p_in:
        copy.wait_recv()
    levels = [stat[0, :4]] + [stat_in[k, :4] for k in (1, 2, 3)]
    best = jnp.maximum(jnp.maximum(levels[0], levels[1]), jnp.maximum(levels[2], levels[3]))
    shares = [jnp.exp2(level - best) for level in levels]
    whole = 1.0 / (shares[0] + shares[1] + shares[2] + shares[3])
    for k in range(4):
        rows = pl.ds(128 * k, 128)
        mixed = jnp.zeros((128, 128), f32)
        for j in range(4):
            share = jnp.transpose(jnp.broadcast_to((shares[j] * whole)[k : k + 1], (128, 128)))
            block = part[0, rows] if j == 0 else part_in[j, rows]
            mixed = mixed + share * block.astype(f32)
        mixed = mixed.astype(bf)
        rows_ref[:, pl.ds(256 * k, 128)] = mixed[:64]
        rows_ref[:, pl.ds(256 * k + 128, 128)] = mixed[64:]

    def product(g):
        return jnp.dot(rows_ref[...], proj[:, pl.ds(pl.multiple_of(g * 896, 128), 896)], preferred_element_type=f32)

    def outward(s):
        return describe(out_part.at[s], out_in.at[me], s_send.at[s], s_recv.at[me], seq_peer(s))

    def inward(s):
        return describe(out_part.at[s], out_in.at[s], s_send.at[s], s_recv.at[s], seq_peer(s))

    def make(g):
        block = product(g).astype(bf)
        out_part[2 * g] = block[:32]
        out_part[2 * g + 1] = block[32:]

    proj_copy.wait()
    make(lax.rem(group + 1, 8))

    def spread(k, _):
        g = lax.rem(group + k, 8)
        outward(2 * g).start()
        outward(2 * g + 1).start()

        @pl.when(k < 7)
        def _():
            make(lax.rem(group + k + 1, 8))

        return 0

    lax.fori_loop(1, 8, spread, 0)
    padded[...] = jnp.zeros_like(padded)
    for side in range(2):

        @pl.when(zl == side)
        def _():
            padded[:, 448 * side : 448 * side + 448] = resid_ref[...].astype(f32)

    mine = product(group) + padded[...]
    first = zl == 0
    near[...] = jnp.where(first, mine[32:], mine[:32])
    partner = {"seq_1": zh * 2 + 1 - zl}
    near_copy = remote(near, near_in, n_sem.at[0], n_sem.at[1], partner)
    stream = jnp.where(first, mine[:32], mine[32:])
    other = group * 2

    def collect(k, total):
        s = lax.rem(other + 1 + k, 16)
        inward(s).wait_recv()
        return total + out_in[s].astype(f32)

    stream = lax.fori_loop(1, 15, collect, stream)
    near_copy.wait_recv()
    stream = stream + near_in[...]

    squares = jnp.sum(stream * stream, axis=1, keepdims=True)
    high = squares.astype(bf)
    low = (squares - high.astype(f32)).astype(bf)
    lane = lax.broadcasted_iota(jnp.int32, (32, 128), 1)
    at = (y, zh, x, c, zl)
    wide[(*at, slice(None), pl.ds(0, 896))] = (stream * gain_ref[:, pl.ds(pl.multiple_of(group * 896, 128), 896)]).astype(bf)
    wide[(*at, slice(None), pl.ds(896, 128))] = jnp.where(lane < 64, high.astype(f32), low.astype(f32)).astype(bf)

    lanes = (pl.ds(0, 384), pl.ds(384, 384), pl.ds(768, 256))
    every = slice(None)
    along = {"x": ("batch_0", x), "y": ("seq_0", y), "z": ("seq_1", z)}

    def turned(axis, by):
        name, own = along[axis]
        return {name: lax.rem(own + by, 4)}

    def view(p, done, pos, half=None):
        py, pz, px = pos["y"], pos["z"], pos["x"]
        iy = every if "y" in done else py
        izh, izl = (every, every) if "z" in done else (pz // 2, lax.rem(pz, 2))
        ix = every if "x" in done else px
        if half is not None:
            if "y" in done:
                iy = pl.ds(2 * half, 2)
            else:
                izh = pl.ds(half, 1)
        return wide.at[iy, izh, ix, pos.get("c", c), izl, :, lanes[p]]

    orders = (("x", "y", "z"), ("y", "z", "x"), ("z", "x", "y"))
    here = {"x": x, "y": y, "z": z}

    def moved(axis, by):
        return {**here, axis: lax.rem(here[axis] + by, 4)}

    pending = []
    hid_own[...] = stream.astype(bf)
    hid_copy = None
    waits = {}
    for stage, (sends, recvs) in enumerate(((g1_send, g1_recv), (g2_send, g2_recv))):
        for p in range(3):
            axis, done = orders[p][stage], orders[p][:stage]
            for k in (1, 3, 2):
                n = p * 3 + k - 1
                own = view(p, done, here)
                copy = remote(own, own, sends.at[n], recvs.at[n], turned(axis, k))
                pending.append(copy)
                waits[stage, p, k] = (done, axis, n, sends, recvs)
        if stage == 0:
            hid_copy = remote(hid_own, hid_in.at[zl], h_sem.at[0], h_sem.at[1], partner)
            hid_in[zl] = hid_own[...]
        for p in range(3):
            done, axis = orders[p][:stage], orders[p][stage]
            for k in (1, 3, 2):
                n = p * 3 + k - 1
                came = view(p, done, moved(axis, 4 - k))
                describe(came, came, sends.at[n], recvs.at[n], turned(axis, k)).wait_recv()
    sibling = {"batch_1": 1 - c}

    def over(p, n, which):
        copy = remote(which, which, c_send.at[n], c_recv.at[n], sibling)
        pending.append(copy)

    for p in range(3):
        axis, done = orders[p][2], orders[p][:2]
        for k, halves in ((1, (0, 1)), (3, (1, 0))):
            for half in halves:
                n = p * 6 + (k // 2) * 2 + half
                own = view(p, done, here, half)
                pending.append(remote(own, own, g3_send.at[n], g3_recv.at[n], turned(axis, k)))
    for p in range(3):
        over(p, p * 4, view(p, orders[p][:2], here))

    def came3(p, k, half):
        axis, done = orders[p][2], orders[p][:2]
        n = p * 6 + {1: 0, 3: 2, 2: 4}[k] + half
        block = view(p, done, moved(axis, 4 - k), half)
        describe(block, block, g3_send.at[n], g3_recv.at[n], turned(axis, 1)).wait_recv()
        return block

    for p in range(3):
        axis = orders[p][2]
        block = came3(p, 1, 0)
        pending.append(remote(block, block, g3_send.at[p * 6 + 4], g3_recv.at[p * 6 + 4], turned(axis, 1)))
        block = came3(p, 3, 1)
        pending.append(remote(block, block, g3_send.at[p * 6 + 5], g3_recv.at[p * 6 + 5], turned(axis, 3)))
    for p in range(3):
        axis, done = orders[p][2], orders[p][:2]
        came3(p, 1, 1)
        over(p, p * 4 + 1, view(p, done, moved(axis, 3)))
        came3(p, 3, 0)
        over(p, p * 4 + 2, view(p, done, moved(axis, 1)))
    for p in range(3):
        axis, done = orders[p][2], orders[p][:2]
        came3(p, 2, 0)
        came3(p, 2, 1)
        over(p, p * 4 + 3, view(p, done, moved(axis, 2)))
    lm_copy.wait()

    def contract(core):
        logits[:, core] = jnp.zeros((4, 64, 512), f32)

        def step(g, squares):
            left = wide[g // 2, lax.rem(g, 2), :, core].reshape(256, 1024)
            right = lm[:, pl.ds(pl.multiple_of(g * 896, 128), 896)]
            added = lax.dot_general(left[:, :896], right, TRANS_B, preferred_element_type=f32)
            logits[:, core] += added.reshape(4, 64, 512)
            return squares + left[:, 896:].astype(f32)

        squares = lax.fori_loop(0, 8, step, jnp.zeros((256, 128), f32))
        rate = lax.rsqrt(jnp.sum(squares, axis=1, keepdims=True) * (1.0 / (64 * 7168)) + norm_epsilon)
        rates[:, core] = jnp.broadcast_to(rate, (256, 128)).reshape(4, 64, 128)

    contract(c)
    for p in range(3):
        axis, done = orders[p][2], orders[p][:2]
        for n, by in ((0, 0), (1, 3), (2, 1), (3, 2)):
            block = view(p, done, {**moved(axis, by), "c": 1 - c})
            describe(block, block, c_send.at[p * 4 + n], c_recv.at[p * 4 + n], sibling).wait_recv()
    contract(1 - c)
    vocab_first = (me * 8 + place) * 512
    entry = lax.broadcasted_iota(jnp.int32, (64, 512), 1) + vocab_first
    spot = lax.broadcasted_iota(jnp.int32, (64, 128), 1)
    tiles[...] = jnp.zeros_like(tiles)

    def column(r):
        return jnp.transpose(jnp.broadcast_to(names[r : r + 1], (128, 128)))[:64].astype(jnp.int32)

    for k in range(4):
        found = [[], [], []]
        for h in range(2):
            parents, wanted = column(2 * k + h), column(8 + 2 * k + h)
            values = logits[k, h] * jnp.tile(rates[k, h], (1, 4))
            best = jnp.max(values, axis=1, keepdims=True)
            mass_here = jnp.sum(jnp.exp(values - best), axis=1, keepdims=True)
            choose = (parents == spot).astype(bf)[:, :64]
            rest, source = values, jnp.zeros((64, 512), f32)
            for _ in range(3):
                piece = rest.astype(bf)
                source = source + jnp.dot(choose, piece, preferred_element_type=f32)
                rest = rest - piece.astype(f32)
            hit = entry == jnp.tile(wanted, (1, 4))
            pick = jnp.sum(jnp.where(hit, source, 0.0), axis=1, keepdims=True)
            for i, one in enumerate((best, mass_here, pick)):
                found[i].append(jnp.broadcast_to(one, (64, 128)))
        for i in range(3):
            line = jnp.transpose(jnp.concatenate(found[i], axis=0))[:8]
            tiles[2 * k, i : i + 1] = line[:1]
            tiles[2 * k + 1, i : i + 1] = pltpu.roll(line, 64, 1)[:1]

    def merge(blocks):
        best = functools.reduce(jnp.maximum, [b[0:1] for b in blocks])
        total = sum(b[1:2] * jnp.exp(b[0:1] - best) for b in blocks)
        return best, total, sum(b[2:3] for b in blocks)

    for k in range(1, 8):
        b = lax.rem(place + k, 8)
        pending.append(remote(tiles.at[b], tile1.at[k], f1_send.at[k], f1_recv.at[k], batch_peer(b)))
    blocks = [tiles[place]]
    for k in range(1, 8):
        describe(tiles.at[0], tile1.at[k], f1_send.at[k], f1_recv.at[k], batch_peer(lax.rem(place + k, 8))).wait_recv()
        blocks.append(tile1[k])
    best, mass_here, pick = merge(blocks)
    merged[...] = jnp.zeros_like(merged)
    merged[0:1] = best
    merged[1:2] = mass_here
    merged[2:3] = pick
    for k in range(1, 16):
        pending.append(remote(merged, tile2.at[k], f2_send.at[k], f2_recv.at[k], seq_peer(lax.rem(me + k, 16))))
    blocks = [merged[...]]
    for k in range(1, 16):
        describe(merged, tile2.at[k], f2_send.at[k], f2_recv.at[k], seq_peer(lax.rem(me + k, 16))).wait_recv()
        blocks.append(tile2[k])
    best, mass_here, pick = merge(blocks)
    log_total = jnp.broadcast_to(best + jnp.log(mass_here), (128, 128))
    lane = lax.broadcasted_iota(jnp.int32, (128, 128), 1)
    own_parents = jnp.sum(jnp.where(own_line, names[0:8], 0.0), axis=0, keepdims=True)
    own_parents = jnp.transpose(jnp.broadcast_to(own_parents, (128, 128))).astype(jnp.int32)
    of_parent = jnp.sum(jnp.where((own_parents == lane) & (lane < 64), log_total, 0.0), axis=1, keepdims=True)
    of_parent = jnp.transpose(jnp.broadcast_to(of_parent, (128, 128)))[:8]
    target = jnp.broadcast_to(pick, (8, 128)) - of_parent
    target_ref[...] = target[:1, :64]
    kept = lane[:8] < jnp.minimum(accept_ref[0], 64)
    score_ref[...] = jnp.sum(jnp.where(kept, target, 0.0), axis=1, keepdims=True)[:1]

    hid_back = describe(hid_own, hid_in.at[1 - zl], h_sem.at[0], h_sem.at[1], partner)
    hid_back.wait_recv()
    for side in range(2):

        @pl.when(zl == side)
        def _():
            for h in range(2):
                hid_ref[32 * h : 32 * h + 32] = hid_in[h, :, 448 * side : 448 * side + 448]

    hid_copy.wait_send()
    near_copy.wait_send()

    def sent(k, _):
        outward(lax.rem(other + 1 + k, 16)).wait_send()
        return 0

    lax.fori_loop(1, 15, sent, 0)
    for copy in pending:
        copy.wait_send()
    for table in (q_in, k_in, r_in, v_in, v_over):
        for copy in table.values():
            copy.wait_send()
    for copy in p_in:
        copy.wait_send()


def whole(scale, cache_len, accept, nope, rope, absorb_k, kl, kr, dl, dr, parent, ids, absorb_v, proj, resid, gain, lm_head):
    bf, f32 = jnp.bfloat16, jnp.float32
    vm, hbm, sm = (pl.BlockSpec(memory_space=space) for space in (pltpu.VMEM, pl.ANY, pltpu.SMEM))
    dma, vmem = pltpu.SemaphoreType.DMA, pltpu.VMEM
    return pl.pallas_call(
        functools.partial(whole_kernel, scale * math.log2(math.e)),
        out_shape=(
            jax.ShapeDtypeStruct((64, 448), bf),
            jax.ShapeDtypeStruct((1, 64), f32),
            jax.ShapeDtypeStruct((1, 1), f32),
        ),
        in_specs=[sm, sm, vm, vm, vm, hbm, hbm, vm, vm, vm, vm, hbm, hbm, vm, vm, hbm],
        out_specs=(vm, vm, vm),
        scratch_shapes=[
            vmem((4, 512, 640), bf), vmem((8, 512, 512), bf), vmem((8, 128, 512), bf), vmem((4, 8, 512, 128), bf),
            vmem((4, 512, 512), f32), vmem((4, 512, 128), f32), vmem((4, 512, 128), f32),
            vmem((4, 512, 128), bf), vmem((4, 512, 128), bf), vmem((4, 8, 128), f32), vmem((4, 8, 128), f32),
            vmem((512, 128), f32), vmem((128, 640), bf), vmem((16, 128), f32), vmem((64, 1024), bf),
            vmem((1024, 7168), bf), vmem((512, 7168), bf), vmem((16, 32, 896), bf), vmem((16, 32, 896), bf),
            vmem((32, 896), f32), vmem((32, 896), f32), vmem((64, 896), f32), vmem((32, 896), bf), vmem((2, 32, 896), bf),
            vmem((4, 2, 4, 2, 2, 32, 1024), bf),
            vmem((4, 2, 64, 512), f32), vmem((4, 2, 64, 128), f32), vmem((8, 8, 128), f32), vmem((8, 128), f32),
            vmem((8, 8, 128), f32), vmem((16, 8, 128), f32),
            dma((7,)), dma((8,)), dma((8,)), dma((8,)), dma((8,)), dma((8,)), dma((8,)),
            dma((11,)), dma((11,)), dma((8,)), dma((8,)),
            dma((16,)), dma((16,)), dma((2,)), dma((2,)), dma((9,)), dma((9,)), dma((9,)), dma((9,)),
            dma((18,)), dma((18,)), dma((12,)), dma((12,)), dma((8,)), dma((8,)), dma((16,)), dma((16,)),
        ],
        compiler_params=pltpu.CompilerParams(collective_id=1, has_side_effects=True, vmem_limit_bytes=57 << 20),
        name="whole",
    )(cache_len, accept, nope, rope, absorb_k, kl, kr, dl, dr, parent, ids, absorb_v, proj, resid, gain, lm_head)


def body(
    q_nope,
    q_rope,
    absorb_k,
    absorb_v,
    cache_latent,
    cache_rope,
    draft_latent,
    draft_rope,
    residual,
    out_proj,
    norm_gain,
    lm_head,
    parent,
    draft_ids,
    cache_len,
    accept_len,
):
    score_scale = 1.0 / math.sqrt(q_nope.shape[3] + q_rope.shape[3])
    hidden, target, score = whole(
        score_scale, cache_len, accept_len, q_nope[0], q_rope[0], absorb_k, cache_latent[0], cache_rope[0].T,
        draft_latent[0], draft_rope[0], parent, draft_ids, absorb_v, out_proj, residual, norm_gain[None], lm_head,
    )
    return (hidden, target, score[0])


def solution(mesh):
    split = Mesh(mesh.devices.reshape(4, 4, 4, 2), ("seq_0", "seq_1", "batch_0", "batch_1"))
    in_specs = (
        P(BATCH, None, SEQ, None),
        P(BATCH, None, SEQ, None),
        P(SEQ, None, None),
        P(SEQ, None, None),
        P(BATCH, SEQ, None),
        P(BATCH, SEQ, None),
        P(BATCH, None, None),
        P(BATCH, None, None),
        P(BATCH, SEQ),
        P(SEQ, None),
        P(),
        P(SEQ_BATCH, None),
        P(),
        P(),
        P(BATCH),
        P(BATCH),
    )
    out_specs = (P(BATCH, SEQ), P(BATCH, None), P(BATCH))
    return jax.shard_map(body, mesh=split, in_specs=in_specs, out_specs=out_specs, check_vma=False)
```

```python
import functools
import math

import jax
import jax.numpy as jnp
from jax import lax
from jax.experimental import pallas as pl
from jax.experimental.pallas import tpu as pltpu
from jax.sharding import Mesh
from jax.sharding import PartitionSpec as P

SEQ = ("seq_0", "seq_1")
BATCH = ("batch_0", "batch_1")
SEQ_BATCH = ("seq_0", "seq_1", "batch_0", "batch_1")

norm_epsilon = 1e-06
MESH_ID = pl.DeviceIdType.MESH
LOWEST = -1e28
MASKED = -1e30
TRANS_B = (((1,), (1,)), ((), ()))


def whole_kernel(scale, len_ref, accept_ref, nope_hbm, rope_hbm, ak_hbm, kl_ref, kr_ref, dl_hbm, dr_hbm, parent_ref, ids_ref,
                 av_ref, proj_ref, resid_hbm, gain_hbm, lm_ref, hid_ref, target_ref, score_ref,
                 qbuf, kbuf, krbuf, avbuf, acc, top, mass, part, part_in, stat, stat_in, lse, tree, names, rows_ref,
                 proj, lm, out_part, out_in, near, near_in, padded, hid_own, hid_in, wide, logits, rates, tiles, merged, tile1, tile2,
                 nope_ref, rope_ref, ak_ref, dl_ref, dr_ref, resid_ref, gain_ref,
                 loc_sem, q_send, q_recv, k_send, k_recv, r_send, r_recv, v_send, v_recv, p_send, p_recv,
                 s_send, s_recv, n_sem, h_sem, g1_send, g1_recv, g2_send, g2_recv, g3_send, g3_recv,
                 c_send, c_recv, f1_send, f1_recv, f2_send, f2_recv):
    y, z = lax.axis_index("seq_0"), lax.axis_index("seq_1")
    x, c = lax.axis_index("batch_0"), lax.axis_index("batch_1")
    zh, zl = z // 2, lax.rem(z, 2)
    me, group, place = y * 4 + z, y * 2 + z // 2, x * 2 + c
    bf, f32 = jnp.bfloat16, jnp.float32
    turn = lambda at, by: lax.rem(at + by, 4)

    def seq_peer(s):
        return {"seq_0": s // 4, "seq_1": lax.rem(s, 4)}

    def batch_peer(b):
        return {"batch_0": b // 2, "batch_1": lax.rem(b, 2)}

    barrier = pltpu.get_barrier_semaphore()

    def greet_seq(k, _):
        pl.semaphore_signal(barrier, inc=1, device_id=seq_peer(lax.rem(me + k, 16)), device_id_type=MESH_ID)
        return 0

    def greet_batch(k, _):
        pl.semaphore_signal(barrier, inc=1, device_id=batch_peer(lax.rem(place + k, 8)), device_id_type=MESH_ID)
        return 0

    lax.fori_loop(1, 16, greet_seq, 0)
    lax.fori_loop(1, 8, greet_batch, 0)

    def describe(src, dst, send, recv, peer):
        return pltpu.make_async_remote_copy(src_ref=src, dst_ref=dst, send_sem=send, recv_sem=recv,
                                            device_id=peer, device_id_type=MESH_ID)

    def remote(*spec):
        copy = describe(*spec)
        copy.start()
        return copy

    def local_copy(src, dst, n):
        copy = pltpu.make_async_copy(src, dst, loc_sem.at[n])
        copy.start()
        return copy

    local = []
    nope_in = [local_copy(nope_hbm, nope_ref, 7), local_copy(rope_hbm, rope_ref, 8), local_copy(ak_hbm, ak_ref, 9)]
    small_in = [local_copy(dl_hbm, dl_ref, 10), local_copy(dr_hbm, dr_ref, 11)]
    late_in = [local_copy(resid_hbm, resid_ref, 12), local_copy(gain_hbm, gain_ref, 13)]
    for h in range(2):
        local.append(local_copy(kl_ref.at[pl.ds(512 * h, 512)], kbuf.at[h], h))
        local.append(local_copy(kr_ref.at[:, pl.ds(512 * h, 512)], krbuf.at[h, pl.ds(0, 64)], 2 + h))
    local_av = local_copy(av_ref, avbuf.at[0], 4)
    pl.semaphore_wait(barrier, 22)
    y_right, y_left, y_far = {"seq_0": turn(y, 1)}, {"seq_0": turn(y, 3)}, {"seq_0": turn(y, 2)}
    z_right, z_left = {"seq_1": turn(z, 1)}, {"seq_1": turn(z, 3)}
    sibling = {"batch_1": 1 - c}
    half = lambda h: pl.ds(256 * h, 256)
    sends = []
    q_in, k_in, r_in = {}, {}, {}
    def key_send(slot, h, peer):
        n = slot * 2 + h
        k_in[n] = remote(kl_ref.at[pl.ds(512 * h, 512)], kbuf.at[n], k_send.at[n], k_recv.at[n], peer)
        r_in[n] = remote(kr_ref.at[:, pl.ds(512 * h, 512)], krbuf.at[n, pl.ds(0, 64)], r_send.at[n], r_recv.at[n], peer)

    key_send(1, 0, z_right)
    key_send(2, 1, z_left)

    for copy in nope_in:
        copy.wait()
    content = jnp.swapaxes(nope_ref[...].astype(f32), 0, 1).astype(bf)
    rotary = jnp.swapaxes(rope_ref[...].astype(f32), 0, 1).astype(bf)
    for h in range(8):
        rows = slice(64 * h, 64 * h + 64)
        qbuf[0, rows, 0:512] = jnp.dot(content[h], ak_ref[h], preferred_element_type=f32).astype(bf)
        qbuf[0, rows, 512:576] = rotary[h]
        qbuf[0, rows, 576:640] = jnp.zeros((64, 64), bf)
    for slot, peer, order in ((1, y_right, (0, 1)), (2, y_left, (1, 0))):
        for h in order:
            n = slot * 2 + h
            q_in[n] = remote(qbuf.at[0, half(h)], qbuf.at[slot, half(h)], q_send.at[n], q_recv.at[n], peer)
    proj_copy = local_copy(proj_ref, proj, 5)
    lm_copy = local_copy(lm_ref, lm, 6)
    acc[...] = jnp.zeros_like(acc)
    top[...] = jnp.full(top.shape, LOWEST, f32)
    mass[...] = jnp.zeros_like(mass)

    names[...] = jnp.zeros_like(names)
    names[0:8, 0:64] = parent_ref[...].astype(f32)
    names[8:16, 0:64] = ids_ref[...].astype(f32)
    own_line = lax.broadcasted_iota(jnp.int32, (8, 128), 0) == place
    own_parents = jnp.sum(jnp.where(own_line, names[0:8], 0.0), axis=0, keepdims=True)
    own_parents = jnp.transpose(jnp.broadcast_to(own_parents, (128, 128))).astype(jnp.int32)
    tree[...] = jnp.zeros_like(tree)
    for copy in small_in:
        copy.wait()
    tree[0:64, 0:512] = dl_ref[...]
    tree[0:64, 512:576] = dr_ref[...]
    for n in range(8):
        krbuf[n, 64:128] = jnp.zeros((64, 512), bf)
    row = lax.broadcasted_iota(jnp.int32, (128, 128), 0)
    col = lax.broadcasted_iota(jnp.int32, (128, 128), 1)
    hop = ((own_parents == col) & (row > 0) & (row < 64)).astype(f32)
    known = (row == col).astype(f32)
    for _ in range(6):
        step = hop.astype(bf)
        known = known + jnp.dot(known.astype(bf), step, preferred_element_type=f32)
        hop = jnp.dot(step, step, preferred_element_type=f32)
    tree_bias = jnp.where((known > 0.5) & (col < 64), 0.0, MASKED)[:64]

    def update(slot, rows, count, find, values, bias):
        width = bias.shape[1]
        at = (slot, pl.ds(rows, count))
        scores = find(qbuf[at]) * scale + bias
        before = top[at]
        now = jnp.maximum(before, jnp.max(scores, axis=1, keepdims=True))
        weights = jnp.exp2(scores - jnp.tile(now, (1, width // 128)))
        fade = jnp.exp2(before - now)
        total = mass[at] * fade
        for k in range(width // 128):
            total = total + weights[:, 128 * k : 128 * k + 128]
        mass[at] = total
        top[at] = now
        acc[at] = acc[at] * jnp.tile(fade, (1, 4)) + jnp.dot(
            weights.astype(bf), values, preferred_element_type=f32
        )

    def tree_scores(query):
        return lax.dot_general(query, tree[...], TRANS_B, preferred_element_type=f32)

    for h in range(8):
        update(0, 64 * h, 64, tree_scores, tree[:, :512], tree_bias)

    def chunks(first, count, slots):
        def chunk(kc, _):
            turn_by = jnp.where(kc // 2 == 0, 0, jnp.where(kc // 2 == 1, 3, jnp.where(kc // 2 == 2, 1, 2)))
            start = (y * 4 + lax.rem(z + turn_by, 4)) * 1024 + lax.rem(kc, 2) * 512
            spot = start + lax.broadcasted_iota(jnp.int32, (1, 512), 1)
            bias = jnp.where(spot < len_ref[0], 0.0, MASKED)
            def cache_scores(query):
                return lax.dot_general(query[:, :512], kbuf[kc], TRANS_B, preferred_element_type=f32) + jnp.dot(
                    query[:, 512:], krbuf[kc], preferred_element_type=f32
                )

            for slot in slots:
                update(slot, 0, 512, cache_scores, kbuf[kc], bias)
            return 0

        lax.fori_loop(first, first + count, chunk, 0)

    for copy in local:
        copy.wait()
    chunks(0, 2, (0,))

    q_in[2].wait_recv()
    q_in[6] = remote(qbuf.at[1, half(0)], qbuf.at[3, half(0)], q_send.at[6], q_recv.at[6], y_right)
    q_in[5].wait_recv()
    q_in[7] = remote(qbuf.at[2, half(1)], qbuf.at[3, half(1)], q_send.at[7], q_recv.at[7], y_left)
    v_in = {}
    mine = 4 * c
    pair = lambda first, h: pl.ds(first + 2 * h, 2)
    for slot, peer, order in ((1, y_right, (0, 1)), (2, y_left, (1, 0))):
        for h in order:
            n = slot * 2 + h
            v_in[n] = remote(av_ref.at[pair(mine, h)], avbuf.at[slot, pair(mine, h)], v_send.at[n], v_recv.at[n], peer)

    def key_wait(n):
        k_in[n].wait_recv()
        r_in[n].wait_recv()

    def key_on(n, m, peer):
        k_in[m] = remote(kbuf.at[n], kbuf.at[m], k_send.at[m], k_recv.at[m], peer)
        r_in[m] = remote(krbuf.at[n, pl.ds(0, 64)], krbuf.at[m, pl.ds(0, 64)], r_send.at[m], r_recv.at[m], peer)

    key_wait(2)
    key_on(2, 6, z_right)
    key_wait(5)
    key_on(5, 7, z_left)
    q_in[3].wait_recv()
    q_in[4].wait_recv()
    chunks(0, 2, (1, 2))
    chunks(2, 1, (0, 1, 2))
    chunks(5, 1, (0, 1, 2))
    q_in[6].wait_recv()
    q_in[7].wait_recv()
    chunks(0, 3, (3,))
    chunks(5, 1, (3,))
    for n in (6, 7):
        k_in[n].wait_send()
        r_in[n].wait_send()
    key_send(1, 1, z_right)
    key_send(2, 0, z_left)
    v_in[2].wait_recv()
    v_in[6] = remote(avbuf.at[1, pair(mine, 0)], avbuf.at[3, pair(mine, 0)], v_send.at[6], v_recv.at[6], y_right)
    v_in[5].wait_recv()
    v_in[7] = remote(avbuf.at[2, pair(mine, 1)], avbuf.at[3, pair(mine, 1)], v_send.at[7], v_recv.at[7], y_left)
    key_wait(6)
    key_wait(7)
    chunks(6, 2, (0, 1, 2, 3))
    v_in[3].wait_recv()
    v_in[4].wait_recv()
    v_over = {}

    def heads_over(slot):
        some = avbuf.at[slot, pl.ds(mine, 4)]
        v_over[slot] = remote(some, some, v_send.at[7 + slot], v_recv.at[7 + slot], sibling)

    heads_over(1)
    heads_over(2)
    v_in[6].wait_recv()
    v_in[7].wait_recv()
    heads_over(3)
    key_wait(3)
    key_wait(4)
    local_av.wait()

    def finish(slot):
        for h in range(8):
            at = (slot, slice(64 * h, 64 * h + 64))
            total = jnp.sum(mass[at], axis=1, keepdims=True)
            some = total > 0.0
            safe = jnp.where(some, total, 1.0)
            value = jnp.dot(acc[at].astype(bf), avbuf[slot, h], preferred_element_type=f32)
            part[at] = (value * jnp.where(some, 1.0 / safe, 0.0)).astype(bf)
            lse[64 * h : 64 * h + 64] = jnp.where(some, top[at] + jnp.log2(safe), LOWEST)
        for k in range(4):
            stat[slot, pl.ds(k, 1)] = jnp.transpose(lse[pl.ds(128 * k, 128)])[:1]

    p_in = []
    for slot, landing, peer in ((1, 2, y_left), (2, 1, y_right), (3, 3, y_far)):
        chunks(3, 2, (slot,))
        v_over[slot].wait_recv()
        finish(slot)
        p_in.append(remote(part.at[slot], part_in.at[landing], p_send.at[landing], p_recv.at[landing], peer))
        p_in.append(remote(stat.at[slot], stat_in.at[landing], p_send.at[landing + 4], p_recv.at[landing + 4], peer))
    chunks(3, 2, (0,))
    finish(0)
    for copy in p_in:
        copy.wait_recv()
    levels = [stat[0, :4]] + [stat_in[k, :4] for k in (1, 2, 3)]
    best = jnp.maximum(jnp.maximum(levels[0], levels[1]), jnp.maximum(levels[2], levels[3]))
    shares = [jnp.exp2(level - best) for level in levels]
    whole = 1.0 / (shares[0] + shares[1] + shares[2] + shares[3])
    for k in range(4):
        rows = pl.ds(128 * k, 128)
        mixed = jnp.zeros((128, 128), f32)
        for j in range(4):
            share = jnp.transpose(jnp.broadcast_to((shares[j] * whole)[k : k + 1], (128, 128)))
            block = part[0, rows] if j == 0 else part_in[j, rows]
            mixed = mixed + share * block.astype(f32)
        mixed = mixed.astype(bf)
        rows_ref[:, pl.ds(256 * k, 128)] = mixed[:64]
        rows_ref[:, pl.ds(256 * k + 128, 128)] = mixed[64:]

    def product(g):
        return jnp.dot(rows_ref[...], proj[:, pl.ds(pl.multiple_of(g * 896, 128), 896)], preferred_element_type=f32)

    def outward(s):
        return describe(out_part.at[s], out_in.at[me], s_send.at[s], s_recv.at[me], seq_peer(s))

    def inward(s):
        return describe(out_part.at[s], out_in.at[s], s_send.at[s], s_recv.at[s], seq_peer(s))

    def make(g):
        block = product(g).astype(bf)
        out_part[2 * g] = block[:32]
        out_part[2 * g + 1] = block[32:]

    proj_copy.wait()
    for copy in late_in:
        copy.wait()
    make(lax.rem(group + 1, 8))

    def spread(k, _):
        g = lax.rem(group + k, 8)
        outward(2 * g).start()
        outward(2 * g + 1).start()

        @pl.when(k < 7)
        def _():
            make(lax.rem(group + k + 1, 8))

        return 0

    lax.fori_loop(1, 8, spread, 0)
    padded[...] = jnp.zeros_like(padded)
    for side in range(2):

        @pl.when(zl == side)
        def _():
            padded[:, 448 * side : 448 * side + 448] = resid_ref[...].astype(f32)

    mine = product(group) + padded[...]
    first = zl == 0
    near[...] = jnp.where(first, mine[32:], mine[:32])
    partner = {"seq_1": zh * 2 + 1 - zl}
    near_copy = remote(near, near_in, n_sem.at[0], n_sem.at[1], partner)
    stream = jnp.where(first, mine[:32], mine[32:])
    other = group * 2

    def collect(k, total):
        s = lax.rem(other + 1 + k, 16)
        inward(s).wait_recv()
        return total + out_in[s].astype(f32)

    stream = lax.fori_loop(1, 15, collect, stream)
    near_copy.wait_recv()
    stream = stream + near_in[...]

    squares = jnp.sum(stream * stream, axis=1, keepdims=True)
    high = squares.astype(bf)
    low = (squares - high.astype(f32)).astype(bf)
    lane = lax.broadcasted_iota(jnp.int32, (32, 128), 1)
    at = (y, zh, x, c, zl)
    wide[(*at, slice(None), pl.ds(0, 896))] = (stream * gain_ref[:, pl.ds(pl.multiple_of(group * 896, 128), 896)]).astype(bf)
    wide[(*at, slice(None), pl.ds(896, 128))] = jnp.where(lane < 64, high.astype(f32), low.astype(f32)).astype(bf)

    lanes = (pl.ds(0, 384), pl.ds(384, 384), pl.ds(768, 256))
    every = slice(None)
    along = {"x": ("batch_0", x), "y": ("seq_0", y), "z": ("seq_1", z)}

    def turned(axis, by):
        name, own = along[axis]
        return {name: lax.rem(own + by, 4)}

    def view(p, done, pos, half=None):
        py, pz, px = pos["y"], pos["z"], pos["x"]
        iy = every if "y" in done else py
        izh, izl = (every, every) if "z" in done else (pz // 2, lax.rem(pz, 2))
        ix = every if "x" in done else px
        if half is not None:
            if "y" in done:
                iy = pl.ds(2 * half, 2)
            else:
                izh = pl.ds(half, 1)
        return wide.at[iy, izh, ix, pos.get("c", c), izl, :, lanes[p]]

    orders = (("x", "y", "z"), ("y", "z", "x"), ("z", "x", "y"))
    here = {"x": x, "y": y, "z": z}

    def moved(axis, by):
        return {**here, axis: lax.rem(here[axis] + by, 4)}

    pending = []
    hid_own[...] = stream.astype(bf)
    stages = ((g1_send, g1_recv), (g2_send, g2_recv))

    def begin(stage, p):
        sends, recvs = stages[stage]
        for k in (1, 3, 2):
            n = p * 3 + k - 1
            own = view(p, orders[p][:stage], here)
            pending.append(remote(own, own, sends.at[n], recvs.at[n], turned(orders[p][stage], k)))

    def await_stage(stage, p):
        sends, recvs = stages[stage]
        axis = orders[p][stage]
        for k in (1, 3, 2):
            n = p * 3 + k - 1
            came = view(p, orders[p][:stage], moved(axis, 4 - k))
            describe(came, came, sends.at[n], recvs.at[n], turned(axis, k)).wait_recv()

    sibling = {"batch_1": 1 - c}

    def over(p, n, which):
        pending.append(remote(which, which, c_send.at[n], c_recv.at[n], sibling))

    for p in range(3):
        begin(0, p)
    hid_copy = remote(hid_own, hid_in.at[zl], h_sem.at[0], h_sem.at[1], partner)
    hid_in[zl] = hid_own[...]
    for p in range(3):
        await_stage(0, p)
        begin(1, p)
    for p in range(3):
        await_stage(1, p)
        axis, done = orders[p][2], orders[p][:2]
        for k, halves in ((1, (0, 1)), (3, (1, 0))):
            for half in halves:
                n = p * 6 + (k // 2) * 2 + half
                own = view(p, done, here, half)
                pending.append(remote(own, own, g3_send.at[n], g3_recv.at[n], turned(axis, k)))
        over(p, p * 4, view(p, done, here))

    def came3(p, k, half):
        axis, done = orders[p][2], orders[p][:2]
        n = p * 6 + {1: 0, 3: 2, 2: 4}[k] + half
        block = view(p, done, moved(axis, 4 - k), half)
        describe(block, block, g3_send.at[n], g3_recv.at[n], turned(axis, 1)).wait_recv()
        return block

    for p in range(3):
        axis = orders[p][2]
        block = came3(p, 1, 0)
        pending.append(remote(block, block, g3_send.at[p * 6 + 4], g3_recv.at[p * 6 + 4], turned(axis, 1)))
        block = came3(p, 3, 1)
        pending.append(remote(block, block, g3_send.at[p * 6 + 5], g3_recv.at[p * 6 + 5], turned(axis, 3)))
    for p in range(3):
        axis, done = orders[p][2], orders[p][:2]
        came3(p, 1, 1)
        over(p, p * 4 + 1, view(p, done, moved(axis, 3)))
        came3(p, 3, 0)
        over(p, p * 4 + 2, view(p, done, moved(axis, 1)))
    for p in range(3):
        axis, done = orders[p][2], orders[p][:2]
        came3(p, 2, 0)
        came3(p, 2, 1)
        over(p, p * 4 + 3, view(p, done, moved(axis, 2)))
    lm_copy.wait()

    def contract(core):
        logits[:, core] = jnp.zeros((4, 64, 512), f32)

        def step(g, squares):
            left = wide[g // 2, lax.rem(g, 2), :, core].reshape(256, 1024)
            right = lm[:, pl.ds(pl.multiple_of(g * 896, 128), 896)]
            added = lax.dot_general(left[:, :896], right, TRANS_B, preferred_element_type=f32)
            logits[:, core] += added.reshape(4, 64, 512)
            return squares + left[:, 896:].astype(f32)

        squares = lax.fori_loop(0, 8, step, jnp.zeros((256, 128), f32))
        rate = lax.rsqrt(jnp.sum(squares, axis=1, keepdims=True) * (1.0 / (64 * 7168)) + norm_epsilon)
        rates[:, core] = jnp.broadcast_to(rate, (256, 128)).reshape(4, 64, 128)

    contract(c)
    for p in range(3):
        axis, done = orders[p][2], orders[p][:2]
        for n, by in ((0, 0), (1, 3), (2, 1), (3, 2)):
            block = view(p, done, {**moved(axis, by), "c": 1 - c})
            describe(block, block, c_send.at[p * 4 + n], c_recv.at[p * 4 + n], sibling).wait_recv()
    contract(1 - c)
    vocab_first = (me * 8 + place) * 512
    entry = lax.broadcasted_iota(jnp.int32, (64, 512), 1) + vocab_first
    spot = lax.broadcasted_iota(jnp.int32, (64, 128), 1)
    tiles[...] = jnp.zeros_like(tiles)

    def column(r):
        return jnp.transpose(jnp.broadcast_to(names[r : r + 1], (128, 128)))[:64].astype(jnp.int32)

    for k in range(4):
        found = [[], [], []]
        for h in range(2):
            parents, wanted = column(2 * k + h), column(8 + 2 * k + h)
            values = logits[k, h] * jnp.tile(rates[k, h], (1, 4))
            best = jnp.max(values, axis=1, keepdims=True)
            mass_here = jnp.sum(jnp.exp(values - best), axis=1, keepdims=True)
            choose = (parents == spot).astype(bf)[:, :64]
            rest, source = values, jnp.zeros((64, 512), f32)
            for _ in range(3):
                piece = rest.astype(bf)
                source = source + jnp.dot(choose, piece, preferred_element_type=f32)
                rest = rest - piece.astype(f32)
            hit = entry == jnp.tile(wanted, (1, 4))
            pick = jnp.sum(jnp.where(hit, source, 0.0), axis=1, keepdims=True)
            for i, one in enumerate((best, mass_here, pick)):
                found[i].append(jnp.broadcast_to(one, (64, 128)))
        for i in range(3):
            line = jnp.transpose(jnp.concatenate(found[i], axis=0))[:8]
            tiles[2 * k, i : i + 1] = line[:1]
            tiles[2 * k + 1, i : i + 1] = pltpu.roll(line, 64, 1)[:1]

    def merge(blocks):
        best = functools.reduce(jnp.maximum, [b[0:1] for b in blocks])
        total = sum(b[1:2] * jnp.exp(b[0:1] - best) for b in blocks)
        return best, total, sum(b[2:3] for b in blocks)

    for k in range(1, 8):
        b = lax.rem(place + k, 8)
        pending.append(remote(tiles.at[b], tile1.at[k], f1_send.at[k], f1_recv.at[k], batch_peer(b)))
    blocks = [tiles[place]]
    for k in range(1, 8):
        describe(tiles.at[0], tile1.at[k], f1_send.at[k], f1_recv.at[k], batch_peer(lax.rem(place + k, 8))).wait_recv()
        blocks.append(tile1[k])
    best, mass_here, pick = merge(blocks)
    merged[...] = jnp.zeros_like(merged)
    merged[0:1] = best
    merged[1:2] = mass_here
    merged[2:3] = pick
    for k in range(1, 16):
        pending.append(remote(merged, tile2.at[k], f2_send.at[k], f2_recv.at[k], seq_peer(lax.rem(me + k, 16))))
    blocks = [merged[...]]
    for k in range(1, 16):
        describe(merged, tile2.at[k], f2_send.at[k], f2_recv.at[k], seq_peer(lax.rem(me + k, 16))).wait_recv()
        blocks.append(tile2[k])
    best, mass_here, pick = merge(blocks)
    log_total = jnp.broadcast_to(best + jnp.log(mass_here), (128, 128))
    lane = lax.broadcasted_iota(jnp.int32, (128, 128), 1)
    own_parents = jnp.sum(jnp.where(own_line, names[0:8], 0.0), axis=0, keepdims=True)
    own_parents = jnp.transpose(jnp.broadcast_to(own_parents, (128, 128))).astype(jnp.int32)
    of_parent = jnp.sum(jnp.where((own_parents == lane) & (lane < 64), log_total, 0.0), axis=1, keepdims=True)
    of_parent = jnp.transpose(jnp.broadcast_to(of_parent, (128, 128)))[:8]
    target = jnp.broadcast_to(pick, (8, 128)) - of_parent
    target_ref[...] = target[:1, :64]
    kept = lane[:8] < jnp.minimum(accept_ref[0], 64)
    score_ref[...] = jnp.sum(jnp.where(kept, target, 0.0), axis=1, keepdims=True)[:1]

    hid_back = describe(hid_own, hid_in.at[1 - zl], h_sem.at[0], h_sem.at[1], partner)
    hid_back.wait_recv()
    for side in range(2):

        @pl.when(zl == side)
        def _():
            for h in range(2):
                hid_ref[32 * h : 32 * h + 32] = hid_in[h, :, 448 * side : 448 * side + 448]

    hid_copy.wait_send()
    near_copy.wait_send()

    def sent(k, _):
        outward(lax.rem(other + 1 + k, 16)).wait_send()
        return 0

    lax.fori_loop(1, 15, sent, 0)
    for copy in pending:
        copy.wait_send()
    for n in (6, 7):
        del k_in[n], r_in[n]
    for table in (q_in, k_in, r_in, v_in, v_over):
        for copy in table.values():
            copy.wait_send()
    for copy in p_in:
        copy.wait_send()


def whole(scale, cache_len, accept, nope, rope, absorb_k, kl, kr, dl, dr, parent, ids, absorb_v, proj, resid, gain, lm_head):
    bf, f32 = jnp.bfloat16, jnp.float32
    vm, hbm, sm = (pl.BlockSpec(memory_space=space) for space in (pltpu.VMEM, pl.ANY, pltpu.SMEM))
    dma, vmem = pltpu.SemaphoreType.DMA, pltpu.VMEM
    return pl.pallas_call(
        functools.partial(whole_kernel, scale * math.log2(math.e)),
        out_shape=(
            jax.ShapeDtypeStruct((64, 448), bf),
            jax.ShapeDtypeStruct((1, 64), f32),
            jax.ShapeDtypeStruct((1, 1), f32),
        ),
        in_specs=[sm, sm, hbm, hbm, hbm, hbm, hbm, hbm, hbm, vm, vm, hbm, hbm, hbm, hbm, hbm],
        out_specs=(vm, vm, vm),
        scratch_shapes=[
            vmem((4, 512, 640), bf), vmem((8, 512, 512), bf), vmem((8, 128, 512), bf), vmem((4, 8, 512, 128), bf),
            vmem((4, 512, 512), f32), vmem((4, 512, 128), f32), vmem((4, 512, 128), f32),
            vmem((4, 512, 128), bf), vmem((4, 512, 128), bf), vmem((4, 8, 128), f32), vmem((4, 8, 128), f32),
            vmem((512, 128), f32), vmem((128, 640), bf), vmem((16, 128), f32), vmem((64, 1024), bf),
            vmem((1024, 7168), bf), vmem((512, 7168), bf), vmem((16, 32, 896), bf), vmem((16, 32, 896), bf),
            vmem((32, 896), f32), vmem((32, 896), f32), vmem((64, 896), f32), vmem((32, 896), bf), vmem((2, 32, 896), bf),
            vmem((4, 2, 4, 2, 2, 32, 1024), bf),
            vmem((4, 2, 64, 512), f32), vmem((4, 2, 64, 128), f32), vmem((8, 8, 128), f32), vmem((8, 128), f32),
            vmem((8, 8, 128), f32), vmem((16, 8, 128), f32),
            vmem((64, 8, 128), bf), vmem((64, 8, 64), bf), vmem((8, 128, 512), bf), vmem((64, 512), bf), vmem((64, 64), bf),
            vmem((64, 448), bf), vmem((1, 7168), f32),
            dma((14,)), dma((8,)), dma((8,)), dma((8,)), dma((8,)), dma((8,)), dma((8,)),
            dma((11,)), dma((11,)), dma((8,)), dma((8,)),
            dma((16,)), dma((16,)), dma((2,)), dma((2,)), dma((9,)), dma((9,)), dma((9,)), dma((9,)),
            dma((18,)), dma((18,)), dma((12,)), dma((12,)), dma((8,)), dma((8,)), dma((16,)), dma((16,)),
        ],
        compiler_params=pltpu.CompilerParams(collective_id=1, has_side_effects=True, vmem_limit_bytes=57 << 20),
        name="whole",
    )(cache_len, accept, nope, rope, absorb_k, kl, kr, dl, dr, parent, ids, absorb_v, proj, resid, gain, lm_head)


def body(
    q_nope,
    q_rope,
    absorb_k,
    absorb_v,
    cache_latent,
    cache_rope,
    draft_latent,
    draft_rope,
    residual,
    out_proj,
    norm_gain,
    lm_head,
    parent,
    draft_ids,
    cache_len,
    accept_len,
):
    score_scale = 1.0 / math.sqrt(q_nope.shape[3] + q_rope.shape[3])
    hidden, target, score = whole(
        score_scale, cache_len, accept_len, q_nope[0], q_rope[0], absorb_k, cache_latent[0], cache_rope[0].T,
        draft_latent[0], draft_rope[0], parent, draft_ids, absorb_v, out_proj, residual, norm_gain[None], lm_head,
    )
    return (hidden, target, score[0])


def solution(mesh):
    split = Mesh(mesh.devices.reshape(4, 4, 4, 2), ("seq_0", "seq_1", "batch_0", "batch_1"))
    in_specs = (
        P(BATCH, None, SEQ, None),
        P(BATCH, None, SEQ, None),
        P(SEQ, None, None),
        P(SEQ, None, None),
        P(BATCH, SEQ, None),
        P(BATCH, SEQ, None),
        P(BATCH, None, None),
        P(BATCH, None, None),
        P(BATCH, SEQ),
        P(SEQ, None),
        P(),
        P(SEQ_BATCH, None),
        P(),
        P(),
        P(BATCH),
        P(BATCH),
    )
    out_specs = (P(BATCH, SEQ), P(BATCH, None), P(BATCH))
    return jax.shard_map(body, mesh=split, in_specs=in_specs, out_specs=out_specs, check_vma=False)
```

```python
import functools
import math

import jax
import jax.numpy as jnp
from jax import lax
from jax.experimental import pallas as pl
from jax.experimental.pallas import tpu as pltpu
from jax.sharding import Mesh
from jax.sharding import PartitionSpec as P

SEQ = ("seq_0", "seq_1")
BATCH = ("batch_0", "batch_1")
SEQ_BATCH = ("seq_0", "seq_1", "batch_0", "batch_1")

norm_epsilon = 1e-06
MESH_ID = pl.DeviceIdType.MESH
LOWEST = -1e28
MASKED = -1e30
TRANS_B = (((1,), (1,)), ((), ()))


def whole_kernel(scale, len_ref, accept_ref, nope_hbm, rope_hbm, ak_hbm, kl_ref, kr_ref, dl_hbm, dr_hbm, parent_ref, ids_ref,
                 av_ref, proj_ref, resid_hbm, gain_hbm, lm_ref, hid_ref, target_ref, score_ref,
                 qbuf, kbuf, krbuf, avbuf, acc, top, mass, part, part_in, stat, stat_in, lse, tree, names, rows_ref,
                 proj, lm, out_part, out_in, near, near_in, padded, hid_own, hid_in, wide, logits, rates, tiles, merged, tile1, tile2,
                 nope_ref, rope_ref, ak_ref, dl_ref, dr_ref, resid_ref, gain_ref,
                 loc_sem, q_send, q_recv, k_send, k_recv, r_send, r_recv, v_send, v_recv, p_send, p_recv,
                 s_send, s_recv, n_sem, h_sem, g1_send, g1_recv, g2_send, g2_recv, g3_send, g3_recv,
                 c_send, c_recv, f1_send, f1_recv, f2_send, f2_recv):
    y, z = lax.axis_index("seq_0"), lax.axis_index("seq_1")
    x, c = lax.axis_index("batch_0"), lax.axis_index("batch_1")
    zh, zl = z // 2, lax.rem(z, 2)
    me, group, place = y * 4 + z, y * 2 + z // 2, x * 2 + c
    bf, f32 = jnp.bfloat16, jnp.float32
    turn = lambda at, by: lax.rem(at + by, 4)

    def seq_peer(s):
        return {"seq_0": s // 4, "seq_1": lax.rem(s, 4)}

    def batch_peer(b):
        return {"batch_0": b // 2, "batch_1": lax.rem(b, 2)}

    barrier = pltpu.get_barrier_semaphore()

    def greet_seq(k, _):
        pl.semaphore_signal(barrier, inc=1, device_id=seq_peer(lax.rem(me + k, 16)), device_id_type=MESH_ID)
        return 0

    def greet_batch(k, _):
        pl.semaphore_signal(barrier, inc=1, device_id=batch_peer(lax.rem(place + k, 8)), device_id_type=MESH_ID)
        return 0

    lax.fori_loop(1, 16, greet_seq, 0)
    lax.fori_loop(1, 8, greet_batch, 0)

    def describe(src, dst, send, recv, peer):
        return pltpu.make_async_remote_copy(src_ref=src, dst_ref=dst, send_sem=send, recv_sem=recv,
                                            device_id=peer, device_id_type=MESH_ID)

    def remote(*spec):
        copy = describe(*spec)
        copy.start()
        return copy

    def local_copy(src, dst, n):
        copy = pltpu.make_async_copy(src, dst, loc_sem.at[n])
        copy.start()
        return copy

    local = []
    nope_in = [local_copy(nope_hbm, nope_ref, 7), local_copy(rope_hbm, rope_ref, 8), local_copy(ak_hbm, ak_ref, 9)]
    small_in = [local_copy(dl_hbm, dl_ref, 10), local_copy(dr_hbm, dr_ref, 11)]
    late_in = [local_copy(resid_hbm, resid_ref, 12), local_copy(gain_hbm, gain_ref, 13)]
    for h in range(2):
        local.append(local_copy(kl_ref.at[pl.ds(512 * h, 512)], kbuf.at[h], h))
        local.append(local_copy(kr_ref.at[:, pl.ds(512 * h, 512)], krbuf.at[h, pl.ds(0, 64)], 2 + h))
    local_av = local_copy(av_ref, avbuf.at[0], 4)
    pl.semaphore_wait(barrier, 22)
    y_right, y_left, y_far = {"seq_0": turn(y, 1)}, {"seq_0": turn(y, 3)}, {"seq_0": turn(y, 2)}
    z_right, z_left = {"seq_1": turn(z, 1)}, {"seq_1": turn(z, 3)}
    sibling = {"batch_1": 1 - c}
    half = lambda h: pl.ds(256 * h, 256)
    sends = []
    q_in, k_in, r_in = {}, {}, {}
    def key_send(slot, h, peer):
        n = slot * 2 + h
        k_in[n] = remote(kl_ref.at[pl.ds(512 * h, 512)], kbuf.at[n], k_send.at[n], k_recv.at[n], peer)
        r_in[n] = remote(kr_ref.at[:, pl.ds(512 * h, 512)], krbuf.at[n, pl.ds(0, 64)], r_send.at[n], r_recv.at[n], peer)

    key_send(1, 0, z_right)
    key_send(2, 1, z_left)

    for copy in nope_in:
        copy.wait()
    content = jnp.swapaxes(nope_ref[...].astype(f32), 0, 1).astype(bf)
    rotary = jnp.swapaxes(rope_ref[...].astype(f32), 0, 1).astype(bf)
    for h in range(8):
        rows = slice(64 * h, 64 * h + 64)
        qbuf[0, rows, 0:512] = jnp.dot(content[h], ak_ref[h], preferred_element_type=f32).astype(bf)
        qbuf[0, rows, 512:576] = rotary[h]
        qbuf[0, rows, 576:640] = jnp.zeros((64, 64), bf)
    for slot, peer, order in ((1, y_right, (0, 1)), (2, y_left, (1, 0))):
        for h in order:
            n = slot * 2 + h
            q_in[n] = remote(qbuf.at[0, half(h)], qbuf.at[slot, half(h)], q_send.at[n], q_recv.at[n], peer)
    proj_copy = local_copy(proj_ref, proj, 5)
    lm_copy = local_copy(lm_ref, lm, 6)
    acc[...] = jnp.zeros_like(acc)
    top[...] = jnp.full(top.shape, LOWEST, f32)
    mass[...] = jnp.zeros_like(mass)

    names[...] = jnp.zeros_like(names)
    names[0:8, 0:64] = parent_ref[...].astype(f32)
    names[8:16, 0:64] = ids_ref[...].astype(f32)
    own_line = lax.broadcasted_iota(jnp.int32, (8, 128), 0) == place
    own_parents = jnp.sum(jnp.where(own_line, names[0:8], 0.0), axis=0, keepdims=True)
    own_parents = jnp.transpose(jnp.broadcast_to(own_parents, (128, 128))).astype(jnp.int32)
    tree[...] = jnp.zeros_like(tree)
    for copy in small_in:
        copy.wait()
    tree[0:64, 0:512] = dl_ref[...]
    tree[0:64, 512:576] = dr_ref[...]
    for n in range(8):
        krbuf[n, 64:128] = jnp.zeros((64, 512), bf)
    row = lax.broadcasted_iota(jnp.int32, (128, 128), 0)
    col = lax.broadcasted_iota(jnp.int32, (128, 128), 1)
    hop = ((own_parents == col) & (row > 0) & (row < 64)).astype(f32)
    known = (row == col).astype(f32)
    for _ in range(6):
        step = hop.astype(bf)
        known = known + jnp.dot(known.astype(bf), step, preferred_element_type=f32)
        hop = jnp.dot(step, step, preferred_element_type=f32)
    tree_bias = jnp.where((known > 0.5) & (col < 64), 0.0, MASKED)[:64]

    def update(slot, rows, count, find, values, bias):
        width = bias.shape[1]
        at = (slot, pl.ds(rows, count))
        scores = find(qbuf[at]) * scale + bias
        before = top[at]
        now = jnp.maximum(before, jnp.max(scores, axis=1, keepdims=True))
        weights = jnp.exp2(scores - jnp.tile(now, (1, width // 128)))
        fade = jnp.exp2(before - now)
        total = mass[at] * fade
        for k in range(width // 128):
            total = total + weights[:, 128 * k : 128 * k + 128]
        mass[at] = total
        top[at] = now
        acc[at] = acc[at] * jnp.tile(fade, (1, 4)) + jnp.dot(
            weights.astype(bf), values, preferred_element_type=f32
        )

    def tree_scores(query):
        return lax.dot_general(query, tree[...], TRANS_B, preferred_element_type=f32)

    for h in range(8):
        update(0, 64 * h, 64, tree_scores, tree[:, :512], tree_bias)

    def chunks(first, count, slots):
        def chunk(kc, _):
            turn_by = jnp.where(kc // 2 == 0, 0, jnp.where(kc // 2 == 1, 3, jnp.where(kc // 2 == 2, 1, 2)))
            start = (y * 4 + lax.rem(z + turn_by, 4)) * 1024 + lax.rem(kc, 2) * 512
            spot = start + lax.broadcasted_iota(jnp.int32, (1, 512), 1)
            bias = jnp.where(spot < len_ref[0], 0.0, MASKED)
            def cache_scores(query):
                return lax.dot_general(query[:, :512], kbuf[kc], TRANS_B, preferred_element_type=f32) + jnp.dot(
                    query[:, 512:], krbuf[kc], preferred_element_type=f32
                )

            for slot in slots:
                update(slot, 0, 512, cache_scores, kbuf[kc], bias)
            return 0

        lax.fori_loop(first, first + count, chunk, 0)

    for copy in local:
        copy.wait()
    chunks(0, 2, (0,))

    q_in[2].wait_recv()
    q_in[6] = remote(qbuf.at[1, half(0)], qbuf.at[3, half(0)], q_send.at[6], q_recv.at[6], y_right)
    q_in[5].wait_recv()
    q_in[7] = remote(qbuf.at[2, half(1)], qbuf.at[3, half(1)], q_send.at[7], q_recv.at[7], y_left)
    v_in = {}
    mine = 4 * c
    pair = lambda first, h: pl.ds(first + 2 * h, 2)
    for slot, peer, order in ((1, y_right, (0, 1)), (2, y_left, (1, 0))):
        for h in order:
            n = slot * 2 + h
            v_in[n] = remote(av_ref.at[pair(mine, h)], avbuf.at[slot, pair(mine, h)], v_send.at[n], v_recv.at[n], peer)

    def key_wait(n):
        k_in[n].wait_recv()
        r_in[n].wait_recv()

    def key_on(n, m, peer):
        k_in[m] = remote(kbuf.at[n], kbuf.at[m], k_send.at[m], k_recv.at[m], peer)
        r_in[m] = remote(krbuf.at[n, pl.ds(0, 64)], krbuf.at[m, pl.ds(0, 64)], r_send.at[m], r_recv.at[m], peer)

    key_wait(2)
    key_on(2, 6, z_right)
    key_wait(5)
    key_on(5, 7, z_left)
    q_in[3].wait_recv()
    q_in[4].wait_recv()
    chunks(0, 2, (1, 2))
    chunks(2, 1, (0, 1, 2))
    chunks(5, 1, (0, 1, 2))
    q_in[6].wait_recv()
    q_in[7].wait_recv()
    chunks(0, 3, (3,))
    chunks(5, 1, (3,))
    for n in (6, 7):
        k_in[n].wait_send()
        r_in[n].wait_send()
    key_send(1, 1, z_right)
    key_send(2, 0, z_left)
    v_in[2].wait_recv()
    v_in[6] = remote(avbuf.at[1, pair(mine, 0)], avbuf.at[3, pair(mine, 0)], v_send.at[6], v_recv.at[6], y_right)
    v_in[5].wait_recv()
    v_in[7] = remote(avbuf.at[2, pair(mine, 1)], avbuf.at[3, pair(mine, 1)], v_send.at[7], v_recv.at[7], y_left)
    key_wait(6)
    key_wait(7)
    chunks(6, 2, (0, 1, 2, 3))
    v_in[3].wait_recv()
    v_in[4].wait_recv()
    v_over = {}

    def heads_over(slot):
        some = avbuf.at[slot, pl.ds(mine, 4)]
        v_over[slot] = remote(some, some, v_send.at[7 + slot], v_recv.at[7 + slot], sibling)

    heads_over(1)
    heads_over(2)
    v_in[6].wait_recv()
    v_in[7].wait_recv()
    heads_over(3)
    key_wait(3)
    key_wait(4)
    local_av.wait()

    def finish(slot):
        for h in range(8):
            at = (slot, slice(64 * h, 64 * h + 64))
            total = jnp.sum(mass[at], axis=1, keepdims=True)
            some = total > 0.0
            safe = jnp.where(some, total, 1.0)
            value = jnp.dot(acc[at].astype(bf), avbuf[slot, h], preferred_element_type=f32)
            part[at] = (value * jnp.where(some, 1.0 / safe, 0.0)).astype(bf)
            lse[64 * h : 64 * h + 64] = jnp.where(some, top[at] + jnp.log2(safe), LOWEST)
        for k in range(4):
            stat[slot, pl.ds(k, 1)] = jnp.transpose(lse[pl.ds(128 * k, 128)])[:1]

    p_in = []
    for slot, landing, peer in ((1, 2, y_left), (2, 1, y_right), (3, 3, y_far)):
        if slot != 2:
            chunks(3, 2, (1, 2) if slot == 1 else (slot,))
        v_over[slot].wait_recv()
        finish(slot)
        p_in.append(remote(part.at[slot], part_in.at[landing], p_send.at[landing], p_recv.at[landing], peer))
        p_in.append(remote(stat.at[slot], stat_in.at[landing], p_send.at[landing + 4], p_recv.at[landing + 4], peer))
    chunks(3, 2, (0,))
    finish(0)
    for copy in p_in:
        copy.wait_recv()
    levels = [stat[0, :4]] + [stat_in[k, :4] for k in (1, 2, 3)]
    best = jnp.maximum(jnp.maximum(levels[0], levels[1]), jnp.maximum(levels[2], levels[3]))
    shares = [jnp.exp2(level - best) for level in levels]
    whole = 1.0 / (shares[0] + shares[1] + shares[2] + shares[3])
    for k in range(4):
        rows = pl.ds(128 * k, 128)
        mixed = jnp.zeros((128, 128), f32)
        for j in range(4):
            share = jnp.transpose(jnp.broadcast_to((shares[j] * whole)[k : k + 1], (128, 128)))
            block = part[0, rows] if j == 0 else part_in[j, rows]
            mixed = mixed + share * block.astype(f32)
        mixed = mixed.astype(bf)
        rows_ref[:, pl.ds(256 * k, 128)] = mixed[:64]
        rows_ref[:, pl.ds(256 * k + 128, 128)] = mixed[64:]

    def product(g):
        return jnp.dot(rows_ref[...], proj[:, pl.ds(pl.multiple_of(g * 896, 128), 896)], preferred_element_type=f32)

    def outward(s):
        return describe(out_part.at[s], out_in.at[me], s_send.at[s], s_recv.at[me], seq_peer(s))

    def inward(s):
        return describe(out_part.at[s], out_in.at[s], s_send.at[s], s_recv.at[s], seq_peer(s))

    def make(g):
        block = product(g).astype(bf)
        out_part[2 * g] = block[:32]
        out_part[2 * g + 1] = block[32:]

    proj_copy.wait()
    for copy in late_in:
        copy.wait()
    make(lax.rem(group + 1, 8))

    def spread(k, _):
        g = lax.rem(group + k, 8)
        outward(2 * g).start()
        outward(2 * g + 1).start()

        @pl.when(k < 7)
        def _():
            make(lax.rem(group + k + 1, 8))

        return 0

    lax.fori_loop(1, 8, spread, 0)
    padded[...] = jnp.zeros_like(padded)
    for side in range(2):

        @pl.when(zl == side)
        def _():
            padded[:, 448 * side : 448 * side + 448] = resid_ref[...].astype(f32)

    mine = product(group) + padded[...]
    first = zl == 0
    near[...] = jnp.where(first, mine[32:], mine[:32])
    partner = {"seq_1": zh * 2 + 1 - zl}
    near_copy = remote(near, near_in, n_sem.at[0], n_sem.at[1], partner)
    stream = jnp.where(first, mine[:32], mine[32:])
    other = group * 2

    def collect(k, total):
        s = lax.rem(other + 1 + k, 16)
        inward(s).wait_recv()
        return total + out_in[s].astype(f32)

    stream = lax.fori_loop(1, 15, collect, stream)
    near_copy.wait_recv()
    stream = stream + near_in[...]

    squares = jnp.sum(stream * stream, axis=1, keepdims=True)
    high = squares.astype(bf)
    low = (squares - high.astype(f32)).astype(bf)
    lane = lax.broadcasted_iota(jnp.int32, (32, 128), 1)
    at = (y, zh, x, c, zl)
    wide[(*at, slice(None), pl.ds(0, 896))] = (stream * gain_ref[:, pl.ds(pl.multiple_of(group * 896, 128), 896)]).astype(bf)
    wide[(*at, slice(None), pl.ds(896, 128))] = jnp.where(lane < 64, high.astype(f32), low.astype(f32)).astype(bf)

    lanes = (pl.ds(0, 384), pl.ds(384, 384), pl.ds(768, 256))
    every = slice(None)
    along = {"x": ("batch_0", x), "y": ("seq_0", y), "z": ("seq_1", z)}

    def turned(axis, by):
        name, own = along[axis]
        return {name: lax.rem(own + by, 4)}

    def view(p, done, pos, half=None):
        py, pz, px = pos["y"], pos["z"], pos["x"]
        iy = every if "y" in done else py
        izh, izl = (every, every) if "z" in done else (pz // 2, lax.rem(pz, 2))
        ix = every if "x" in done else px
        if half is not None:
            if "y" in done:
                iy = pl.ds(2 * half, 2)
            else:
                izh = pl.ds(half, 1)
        return wide.at[iy, izh, ix, pos.get("c", c), izl, :, lanes[p]]

    orders = (("x", "y", "z"), ("y", "z", "x"), ("z", "x", "y"))
    here = {"x": x, "y": y, "z": z}

    def moved(axis, by):
        return {**here, axis: lax.rem(here[axis] + by, 4)}

    pending = []
    hid_own[...] = stream.astype(bf)
    stages = ((g1_send, g1_recv), (g2_send, g2_recv))

    def begin(stage, p):
        sends, recvs = stages[stage]
        for k in (1, 3, 2):
            n = p * 3 + k - 1
            own = view(p, orders[p][:stage], here)
            pending.append(remote(own, own, sends.at[n], recvs.at[n], turned(orders[p][stage], k)))

    def await_stage(stage, p):
        sends, recvs = stages[stage]
        axis = orders[p][stage]
        for k in (1, 3, 2):
            n = p * 3 + k - 1
            came = view(p, orders[p][:stage], moved(axis, 4 - k))
            describe(came, came, sends.at[n], recvs.at[n], turned(axis, k)).wait_recv()

    sibling = {"batch_1": 1 - c}

    def over(p, n, which):
        pending.append(remote(which, which, c_send.at[n], c_recv.at[n], sibling))

    for p in range(3):
        begin(0, p)
    hid_copy = remote(hid_own, hid_in.at[zl], h_sem.at[0], h_sem.at[1], partner)
    hid_in[zl] = hid_own[...]
    for p in range(3):
        await_stage(0, p)
        begin(1, p)
    for p in range(3):
        await_stage(1, p)
        axis, done = orders[p][2], orders[p][:2]
        for k, halves in ((1, (0, 1)), (3, (1, 0))):
            for half in halves:
                n = p * 6 + (k // 2) * 2 + half
                own = view(p, done, here, half)
                pending.append(remote(own, own, g3_send.at[n], g3_recv.at[n], turned(axis, k)))
        over(p, p * 4, view(p, done, here))

    def came3(p, k, half):
        axis, done = orders[p][2], orders[p][:2]
        n = p * 6 + {1: 0, 3: 2, 2: 4}[k] + half
        block = view(p, done, moved(axis, 4 - k), half)
        describe(block, block, g3_send.at[n], g3_recv.at[n], turned(axis, 1)).wait_recv()
        return block

    for p in range(3):
        axis = orders[p][2]
        block = came3(p, 1, 0)
        pending.append(remote(block, block, g3_send.at[p * 6 + 4], g3_recv.at[p * 6 + 4], turned(axis, 1)))
        block = came3(p, 3, 1)
        pending.append(remote(block, block, g3_send.at[p * 6 + 5], g3_recv.at[p * 6 + 5], turned(axis, 3)))
    for p in range(3):
        axis, done = orders[p][2], orders[p][:2]
        came3(p, 1, 1)
        over(p, p * 4 + 1, view(p, done, moved(axis, 3)))
        came3(p, 3, 0)
        over(p, p * 4 + 2, view(p, done, moved(axis, 1)))
    for p in range(3):
        axis, done = orders[p][2], orders[p][:2]
        came3(p, 2, 0)
        came3(p, 2, 1)
        over(p, p * 4 + 3, view(p, done, moved(axis, 2)))
    lm_copy.wait()

    def contract(core):
        logits[:, core] = jnp.zeros((4, 64, 512), f32)

        def step(g, squares):
            left = wide[g // 2, lax.rem(g, 2), :, core].reshape(256, 1024)
            right = lm[:, pl.ds(pl.multiple_of(g * 896, 128), 896)]
            added = lax.dot_general(left[:, :896], right, TRANS_B, preferred_element_type=f32)
            logits[:, core] += added.reshape(4, 64, 512)
            return squares + left[:, 896:].astype(f32)

        squares = lax.fori_loop(0, 8, step, jnp.zeros((256, 128), f32))
        rate = lax.rsqrt(jnp.sum(squares, axis=1, keepdims=True) * (1.0 / (64 * 7168)) + norm_epsilon)
        rates[:, core] = jnp.broadcast_to(rate, (256, 128)).reshape(4, 64, 128)

    vocab_first = (me * 8 + place) * 512
    entry = lax.broadcasted_iota(jnp.int32, (64, 512), 1) + vocab_first
    spot = lax.broadcasted_iota(jnp.int32, (64, 128), 1)
    tiles[...] = jnp.zeros_like(tiles)

    def column(r):
        return jnp.transpose(jnp.broadcast_to(names[pl.ds(r, 1)], (128, 128)))[:64].astype(jnp.int32)

    def summarise(core):
        for k in range(4):
            b = 2 * k + core
            parents, wanted = column(b), column(8 + b)
            values = logits[k, core] * jnp.tile(rates[k, core], (1, 4))
            best = jnp.max(values, axis=1, keepdims=True)
            mass_here = jnp.sum(jnp.exp(values - best), axis=1, keepdims=True)
            choose = (parents == spot).astype(bf)[:, :64]
            rest, source = values, jnp.zeros((64, 512), f32)
            for _ in range(3):
                piece = rest.astype(bf)
                source = source + jnp.dot(choose, piece, preferred_element_type=f32)
                rest = rest - piece.astype(f32)
            hit = entry == jnp.tile(wanted, (1, 4))
            pick = jnp.sum(jnp.where(hit, source, 0.0), axis=1, keepdims=True)
            for i, one in enumerate((best, mass_here, pick)):
                square = jnp.concatenate([jnp.broadcast_to(one, (64, 128)), jnp.zeros((64, 128), f32)], axis=0)
                tiles[b, i : i + 1] = jnp.transpose(square)[:1]

    contract(c)
    summarise(c)
    for p in range(3):
        axis, done = orders[p][2], orders[p][:2]
        for n, by in ((0, 0), (1, 3), (2, 1), (3, 2)):
            block = view(p, done, {**moved(axis, by), "c": 1 - c})
            describe(block, block, c_send.at[p * 4 + n], c_recv.at[p * 4 + n], sibling).wait_recv()
    contract(1 - c)
    summarise(1 - c)

    def merge(blocks):
        best = functools.reduce(jnp.maximum, [b[0:1] for b in blocks])
        total = sum(b[1:2] * jnp.exp(b[0:1] - best) for b in blocks)
        return best, total, sum(b[2:3] for b in blocks)

    for k in range(1, 8):
        b = lax.rem(place + k, 8)
        pending.append(remote(tiles.at[b], tile1.at[k], f1_send.at[k], f1_recv.at[k], batch_peer(b)))
    blocks = [tiles[place]]
    for k in range(1, 8):
        describe(tiles.at[0], tile1.at[k], f1_send.at[k], f1_recv.at[k], batch_peer(lax.rem(place + k, 8))).wait_recv()
        blocks.append(tile1[k])
    best, mass_here, pick = merge(blocks)
    merged[...] = jnp.zeros_like(merged)
    merged[0:1] = best
    merged[1:2] = mass_here
    merged[2:3] = pick
    for k in range(1, 16):
        pending.append(remote(merged, tile2.at[k], f2_send.at[k], f2_recv.at[k], seq_peer(lax.rem(me + k, 16))))
    blocks = [merged[...]]
    for k in range(1, 16):
        describe(merged, tile2.at[k], f2_send.at[k], f2_recv.at[k], seq_peer(lax.rem(me + k, 16))).wait_recv()
        blocks.append(tile2[k])
    best, mass_here, pick = merge(blocks)
    log_total = jnp.broadcast_to(best + jnp.log(mass_here), (128, 128))
    lane = lax.broadcasted_iota(jnp.int32, (128, 128), 1)
    own_parents = jnp.sum(jnp.where(own_line, names[0:8], 0.0), axis=0, keepdims=True)
    own_parents = jnp.transpose(jnp.broadcast_to(own_parents, (128, 128))).astype(jnp.int32)
    of_parent = jnp.sum(jnp.where((own_parents == lane) & (lane < 64), log_total, 0.0), axis=1, keepdims=True)
    of_parent = jnp.transpose(jnp.broadcast_to(of_parent, (128, 128)))[:8]
    target = jnp.broadcast_to(pick, (8, 128)) - of_parent
    target_ref[...] = target[:1, :64]
    kept = lane[:8] < jnp.minimum(accept_ref[0], 64)
    score_ref[...] = jnp.sum(jnp.where(kept, target, 0.0), axis=1, keepdims=True)[:1]

    hid_back = describe(hid_own, hid_in.at[1 - zl], h_sem.at[0], h_sem.at[1], partner)
    hid_back.wait_recv()
    for side in range(2):

        @pl.when(zl == side)
        def _():
            for h in range(2):
                hid_ref[32 * h : 32 * h + 32] = hid_in[h, :, 448 * side : 448 * side + 448]

    hid_copy.wait_send()
    near_copy.wait_send()

    def sent(k, _):
        outward(lax.rem(other + 1 + k, 16)).wait_send()
        return 0

    lax.fori_loop(1, 15, sent, 0)
    for copy in pending:
        copy.wait_send()
    for n in (6, 7):
        del k_in[n], r_in[n]
    for table in (q_in, k_in, r_in, v_in, v_over):
        for copy in table.values():
            copy.wait_send()
    for copy in p_in:
        copy.wait_send()


def whole(scale, cache_len, accept, nope, rope, absorb_k, kl, kr, dl, dr, parent, ids, absorb_v, proj, resid, gain, lm_head):
    bf, f32 = jnp.bfloat16, jnp.float32
    vm, hbm, sm = (pl.BlockSpec(memory_space=space) for space in (pltpu.VMEM, pl.ANY, pltpu.SMEM))
    dma, vmem = pltpu.SemaphoreType.DMA, pltpu.VMEM
    return pl.pallas_call(
        functools.partial(whole_kernel, scale * math.log2(math.e)),
        out_shape=(
            jax.ShapeDtypeStruct((64, 448), bf),
            jax.ShapeDtypeStruct((1, 64), f32),
            jax.ShapeDtypeStruct((1, 1), f32),
        ),
        in_specs=[sm, sm, hbm, hbm, hbm, hbm, hbm, hbm, hbm, vm, vm, hbm, hbm, hbm, hbm, hbm],
        out_specs=(vm, vm, vm),
        scratch_shapes=[
            vmem((4, 512, 640), bf), vmem((8, 512, 512), bf), vmem((8, 128, 512), bf), vmem((4, 8, 512, 128), bf),
            vmem((4, 512, 512), f32), vmem((4, 512, 128), f32), vmem((4, 512, 128), f32),
            vmem((4, 512, 128), bf), vmem((4, 512, 128), bf), vmem((4, 8, 128), f32), vmem((4, 8, 128), f32),
            vmem((512, 128), f32), vmem((128, 640), bf), vmem((16, 128), f32), vmem((64, 1024), bf),
            vmem((1024, 7168), bf), vmem((512, 7168), bf), vmem((16, 32, 896), bf), vmem((16, 32, 896), bf),
            vmem((32, 896), f32), vmem((32, 896), f32), vmem((64, 896), f32), vmem((32, 896), bf), vmem((2, 32, 896), bf),
            vmem((4, 2, 4, 2, 2, 32, 1024), bf),
            vmem((4, 2, 64, 512), f32), vmem((4, 2, 64, 128), f32), vmem((8, 8, 128), f32), vmem((8, 128), f32),
            vmem((8, 8, 128), f32), vmem((16, 8, 128), f32),
            vmem((64, 8, 128), bf), vmem((64, 8, 64), bf), vmem((8, 128, 512), bf), vmem((64, 512), bf), vmem((64, 64), bf),
            vmem((64, 448), bf), vmem((1, 7168), f32),
            dma((14,)), dma((8,)), dma((8,)), dma((8,)), dma((8,)), dma((8,)), dma((8,)),
            dma((11,)), dma((11,)), dma((8,)), dma((8,)),
            dma((16,)), dma((16,)), dma((2,)), dma((2,)), dma((9,)), dma((9,)), dma((9,)), dma((9,)),
            dma((18,)), dma((18,)), dma((12,)), dma((12,)), dma((8,)), dma((8,)), dma((16,)), dma((16,)),
        ],
        compiler_params=pltpu.CompilerParams(collective_id=1, has_side_effects=True, vmem_limit_bytes=57 << 20),
        name="whole",
    )(cache_len, accept, nope, rope, absorb_k, kl, kr, dl, dr, parent, ids, absorb_v, proj, resid, gain, lm_head)


def body(
    q_nope,
    q_rope,
    absorb_k,
    absorb_v,
    cache_latent,
    cache_rope,
    draft_latent,
    draft_rope,
    residual,
    out_proj,
    norm_gain,
    lm_head,
    parent,
    draft_ids,
    cache_len,
    accept_len,
):
    score_scale = 1.0 / math.sqrt(q_nope.shape[3] + q_rope.shape[3])
    hidden, target, score = whole(
        score_scale, cache_len, accept_len, q_nope[0], q_rope[0], absorb_k, cache_latent[0], cache_rope[0].T,
        draft_latent[0], draft_rope[0], parent, draft_ids, absorb_v, out_proj, residual, norm_gain[None], lm_head,
    )
    return (hidden, target, score[0])


def solution(mesh):
    split = Mesh(mesh.devices.reshape(4, 4, 4, 2), ("seq_0", "seq_1", "batch_0", "batch_1"))
    in_specs = (
        P(BATCH, None, SEQ, None),
        P(BATCH, None, SEQ, None),
        P(SEQ, None, None),
        P(SEQ, None, None),
        P(BATCH, SEQ, None),
        P(BATCH, SEQ, None),
        P(BATCH, None, None),
        P(BATCH, None, None),
        P(BATCH, SEQ),
        P(SEQ, None),
        P(),
        P(SEQ_BATCH, None),
        P(),
        P(),
        P(BATCH),
        P(BATCH),
    )
    out_specs = (P(BATCH, SEQ), P(BATCH, None), P(BATCH))
    return jax.shard_map(body, mesh=split, in_specs=in_specs, out_specs=out_specs, check_vma=False)
```
